32 devices in a mesh: groups: 2 (over y), wave: 4 (over z), section: 4 (over x, core).
Axes of the slice: x: 2, y: 2, z: 4, core: 2. Of those that a mesh axis runs over, the one named last changes fastest.
Arguments:
- nominal_field: float32 [4, 2, 1024], P('wave'), may hold values from -6 to 6
- sensitivity: bfloat16 [4, 360, 2, 1024], P('wave'), may hold values from -0.3125 to 0.3125
- aberrations: bfloat16 [128, 360], P('groups'), parts along dimension 0, may hold values from -13 to 13
- jacobian: bfloat16 [4, 2, 1024, 8192], P('wave', None, None, 'section'), may hold values from -1 to 1
- tile_mask: int32 [4, 8], P('wave'), may hold values 0 or 1
- regul: float32 [8192], P('section'), may hold values from 0.05 to 0.5
- initial_commands: float32 [128, 8192], P('groups', 'section'), parts along dimension 0, may hold values from -3 to 3
Outputs:
- commands: float32 [128, 8192], P('groups', 'section'), parts along dimension 0
- dark_field: float32 [128, 4, 2, 1024], P('groups', 'wave'), parts along dimension 0
The draws below stay inside these ranges and needn't reach their ends.
There are 2 independent parts, one for each index of `groups`. The reference program is written for one: setup_inputs(seed, part) draws one part's arguments, and reference() takes and returns one part's arrays. A program takes and returns all parts, laid end to end along the dimension named above; an argument that names none is the same for every part. Nothing has to cross between parts.
All inputs are finite; a program needn't handle non-finite values. No bound on the sum of `tile_mask` on one device may be relied on, other than what follows from the above.
Results may differ from the reference program's by a relative error of at most 0.035.
Values may be sent and summed in bfloat16 or wider, within the bound.
A program may use at most 64 MiB of HBM per device.

```python
import math
import jax
import jax.numpy as jnp
from jax import lax

ACT = 8192
MODES = 360
TILE = 128
TILES = 8
ITERS = 2
CG = 5
PIX = 1024
REALS = 64
WAVES = 4
ACT_DEV = 2048
N_SECTION = 4


def draw_jacobian(key, part):
    column = jnp.arange(ACT, dtype=jnp.float32) / ACT
    raw = jnp.clip(jax.random.normal(key, (WAVES, 2, PIX, ACT), jnp.float32), -4.0, 4.0)
    scale = 10.0 ** (column - 0.5)
    return jnp.clip(raw * scale * ACT ** (-0.5), -1.0, 1.0).astype(jnp.bfloat16)


def draw_aberrations(key, part):
    first_key, second_key = jax.random.split(jax.random.fold_in(key, 7))
    level = jax.random.uniform(first_key, (REALS, 1), jnp.float32, -0.5, 0.5)
    raw = jnp.clip(jax.random.normal(second_key, (REALS, MODES), jnp.float32), -4.0, 4.0)
    scale = 10.0 ** level
    return (raw * scale).astype(jnp.bfloat16)


def touch_ends(values, rng, smallest, largest):
    index_at = [jax.random.randint(jax.random.fold_in(rng, axis), (), 0, length) for axis, length in enumerate(values.shape)]
    longest = values.shape.index(max(values.shape))
    next_to = index_at[:longest] + [(index_at[longest] + 1) % values.shape[longest]] + index_at[longest + 1:]
    return values.at[tuple(index_at)].set(smallest).at[tuple(next_to)].set(largest)


def level_of(own_key, shape, cuts, low, largest):
    level = 1.0
    for axis_at, parts in cuts:
        heights = jax.random.uniform(jax.random.fold_in(jax.random.fold_in(own_key, 6), axis_at), (parts,), jnp.float32, low / len(cuts), largest / len(cuts))
        level = level * jnp.repeat(jnp.exp(heights), shape[axis_at] // parts).reshape((-1,) + (1,) * (len(shape) - 1 - axis_at))
    return level


def scatter_about(rng, extent, deviation, limit, cuts=(), kind=jnp.bfloat16):
    level = level_of(rng, extent, cuts, -0.22, 0.18) if cuts else 1.0
    values = jax.random.normal(rng, extent, jnp.float32) * deviation * level
    return jnp.minimum(jnp.maximum(values, -limit), limit).astype(kind)


def setup_inputs(seed: int = 0, part: int = 0) -> dict:
    arg_keys = jax.random.split(jax.random.key(seed), 8)
    part_keys = jax.random.split(jax.random.fold_in(arg_keys[7], part), 8)
    return {
        "nominal_field": scatter_about(arg_keys[0], (WAVES, 2, PIX), 1.0, 6.0, ((0, 4),), jnp.float32),
        "sensitivity": scatter_about(arg_keys[1], (WAVES, MODES, 2, PIX), MODES ** -0.5, 0.3125, ((0, 4),)),
        "aberrations": draw_aberrations(jax.random.fold_in(jax.random.fold_in(arg_keys[7], part), 71), part),
        "jacobian": draw_jacobian(jax.random.fold_in(arg_keys[7], 71), part),
        "tile_mask": touch_ends((jax.random.randint(arg_keys[4], (WAVES, TILES), 0, 4) < 3).astype(jnp.int32), jax.random.fold_in(arg_keys[4], 1), 0, 1),
        "regul": jnp.clip(jnp.exp(math.log(0.5) - 2.3025851 * jax.random.uniform(arg_keys[5], (ACT,), jnp.float32) ** level_of(arg_keys[5], (ACT,), ((0, 4),), -0.2, 0.2)), 0.05, 0.5),
        "initial_commands": scatter_about(part_keys[6], (REALS, ACT), 0.5, 3.0, ((1, 4),), jnp.float32),
    }


epsilon = 1e-6


def image_of(command_bf, flat_jac):
    def advance(total_sum, block_index):
        offset = block_index * ACT_DEV
        jac_cols = lax.dynamic_slice_in_dim(flat_jac, offset, ACT_DEV, 1)
        command_cols = lax.dynamic_slice_in_dim(command_bf, offset, ACT_DEV, 1)
        partial_value = jnp.dot(command_cols, jac_cols.T, preferred_element_type=jnp.float32)
        partial_value = lax.optimization_barrier(partial_value.astype(jnp.bfloat16)).astype(jnp.float32)
        return total_sum + partial_value, None

    start_sum = jnp.zeros((command_bf.shape[0], flat_jac.shape[0]), jnp.float32)
    result, _ = lax.scan(advance, start_sum, jnp.arange(N_SECTION, dtype=jnp.int32))
    return result


def back_of(masked_bf, flat_jac):
    span = 2 * PIX

    def advance(total_sum, wave_index):
        offset = wave_index * span
        jac_rows = lax.dynamic_slice_in_dim(flat_jac, offset, span, 0)
        field_rows = lax.dynamic_slice_in_dim(masked_bf, offset, span, 1)
        partial_value = jnp.dot(field_rows, jac_rows, preferred_element_type=jnp.float32)
        partial_value = lax.optimization_barrier(partial_value.astype(jnp.bfloat16)).astype(jnp.float32)
        return total_sum + partial_value, None

    start_sum = jnp.zeros((masked_bf.shape[0], ACT), jnp.float32)
    result, _ = lax.scan(advance, start_sum, jnp.arange(WAVES, dtype=jnp.int32))
    return result


def reference(nominal_field, sensitivity, aberrations, jacobian, tile_mask, regul, initial_commands):
    rows_all = WAVES * 2 * PIX
    flat_jac = jacobian.reshape(rows_all, ACT)
    weight = jnp.broadcast_to(tile_mask.astype(jnp.float32)[:, None, :, None], (WAVES, 2, TILES, TILE)).reshape(1, rows_all)
    sens_rows = jnp.transpose(sensitivity, (1, 0, 2, 3)).reshape(MODES, rows_all)
    field_now = nominal_field.reshape(1, rows_all) + jnp.dot(aberrations, sens_rows, preferred_element_type=jnp.float32)
    commands = initial_commands
    field_now = field_now + image_of(commands.astype(jnp.bfloat16), flat_jac)
    for iteration in range(ITERS):
        residual = -back_of((weight * field_now).astype(jnp.bfloat16), flat_jac)
        direction = residual
        change = jnp.zeros_like(residual)
        field_step = jnp.zeros_like(field_now)
        norm_now = jnp.sum(residual * residual, axis=1)
        for inner_step in range(CG):
            image_now = image_of(direction.astype(jnp.bfloat16), flat_jac)
            applied = back_of((weight * image_now).astype(jnp.bfloat16), flat_jac) + regul[None, :] * direction
            curvature = jnp.sum(direction * applied, axis=1)
            step_len = norm_now / (curvature + epsilon)
            change = change + step_len[:, None] * direction
            field_step = field_step + step_len[:, None] * image_now
            residual = residual - step_len[:, None] * applied
            norm_next = jnp.sum(residual * residual, axis=1)
            direction = residual + (norm_next / (norm_now + epsilon))[:, None] * direction
            norm_now = norm_next
        commands = commands + change
        field_now = field_now + field_step
    return commands, field_now.reshape(REALS, WAVES, 2, PIX)
```

```python
import functools

import jax
import jax.numpy as jnp
from jax import lax
from jax.experimental import pallas as pl
from jax.experimental.pallas import tpu as pltpu
from jax.sharding import PartitionSpec as P

ITERS = 2
CG = 5
LANES = 128
CHUNKS = 2
STREAMS = 2
OWNERS = 2
SIDE = 128

epsilon = 1e-06


def to_section_image(command_bf, jac_block):
    partial_value = lax.dot_general(
        command_bf, jac_block, (((1,), (1,)), ((), ())), preferred_element_type=jnp.float32
    )
    return lax.psum_scatter(
        partial_value.astype(jnp.bfloat16), "section", scatter_dimension=1, tiled=True
    ).astype(jnp.float32)


def back_of(masked_share, jac_block):
    masked_bf = lax.all_gather(masked_share, "section", axis=1, tiled=True)
    partial_value = jnp.dot(masked_bf, jac_block, preferred_element_type=jnp.float32)
    owned = lax.psum_scatter(
        partial_value.astype(jnp.bfloat16), "wave", scatter_dimension=1, tiled=True
    ).astype(jnp.float32)
    return lax.all_gather(owned, "wave", axis=1, tiled=True)


def reduce_scalars(values):
    return lax.psum(values, "section")


def general_shards(nominal_field, sensitivity, aberrations, jacobian, tile_mask, regul, initial_commands):
    components = jacobian.shape[1]
    pixels = jacobian.shape[2]
    block_width = jacobian.shape[3]
    row_count = components * pixels
    share_rows = row_count // lax.axis_size("section")
    row_start = lax.axis_index("section") * share_rows
    jac_block = jacobian.reshape(row_count, block_width)
    tile_count = tile_mask.shape[1]
    weight_full = jnp.broadcast_to(
        tile_mask[0].astype(jnp.float32)[None, :, None],
        (components, tile_count, pixels // tile_count),
    ).reshape(1, row_count)
    weight = lax.dynamic_slice_in_dim(weight_full, row_start, share_rows, 1)
    mode_count = sensitivity.shape[1]
    sens_share = lax.dynamic_slice_in_dim(
        sensitivity.reshape(mode_count, row_count), row_start, share_rows, 1
    )
    nominal_share = lax.dynamic_slice_in_dim(
        nominal_field.reshape(1, row_count), row_start, share_rows, 1
    )
    field_now = nominal_share + jnp.dot(aberrations, sens_share, preferred_element_type=jnp.float32)
    commands = initial_commands
    field_now = field_now + to_section_image(commands.astype(jnp.bfloat16), jac_block)
    for iteration in range(ITERS):
        residual = -back_of((weight * field_now).astype(jnp.bfloat16), jac_block)
        direction = residual
        change = jnp.zeros_like(residual)
        field_step = jnp.zeros_like(field_now)
        norm_now = reduce_scalars(jnp.sum(residual * residual, axis=1))
        for inner_step in range(CG):
            image_now = to_section_image(direction.astype(jnp.bfloat16), jac_block)
            applied = (
                back_of((weight * image_now).astype(jnp.bfloat16), jac_block)
                + regul[None, :] * direction
            )
            curvature = reduce_scalars(jnp.sum(direction * applied, axis=1))
            step_len = norm_now / (curvature + epsilon)
            residual = residual - step_len[:, None] * applied
            norm_next = reduce_scalars(jnp.sum(residual * residual, axis=1))
            change = change + step_len[:, None] * direction
            field_step = field_step + step_len[:, None] * image_now
            direction = residual + (norm_next / (norm_now + epsilon))[:, None] * direction
            norm_now = norm_next
        commands = commands + change
        field_now = field_now + field_step
    whole_field = lax.all_gather(
        field_now.astype(jnp.bfloat16), "section", axis=1, tiled=True
    ).astype(field_now.dtype)
    return (commands, whole_field.reshape(whole_field.shape[0], 1, components, pixels))


def control_kernel(
    n,
    jac_hbm,
    base_ref,
    start_ref,
    regul_ref,
    weight_ref,
    cmd_ref,
    out_ref,
    jac,
    jact,
    probe,
    wpart,
    wrecv,
    ipart,
    crecv,
    xsend,
    xrecv,
    masked,
    img,
    field,
    qown,
    direction,
    change,
    residual,
    acc,
    gamma,
    rho,
    kappas,
    other,
    jac_sem,
    cs_s,
    cs_r,
    xx_s,
    xx_r,
    cg_s,
    cg_r,
    ws_s,
    ws_r,
    ag_s,
    ag_r,
    fin_s,
    fin_r,
    out_s,
    out_r,
):
    f32, bf16 = jnp.float32, jnp.bfloat16
    half, acts = jac.shape[1:]
    mo = probe.shape[2]
    m = OWNERS * mo
    ac = acts // CHUNKS
    last = ITERS * CG
    sec, wav = lax.axis_index("section"), lax.axis_index("wave")
    core = lax.rem(sec, 2)
    sibling = {"section": sec + 1 - 2 * core}
    across = {"section": lax.rem(sec + 2, n)}
    first_owner = n // 2 - 1
    owners = [first_owner + o for o in range(OWNERS)]
    is_owner = jnp.logical_and(wav >= owners[0], wav <= owners[-1])
    mine = jnp.clip(wav - first_owner, 0, OWNERS - 1)
    peers = range(n - 1)
    wav_peer = [{"wave": lax.rem(wav + k + 1, n)} for k in peers]

    loads = []
    for side in range(2):
        at = pl.multiple_of((core if side == 0 else 1 - core) * half, half)
        loads.append(
            pltpu.make_async_copy(jac_hbm.at[pl.ds(at, half)], jac.at[side], jac_sem.at[side])
        )
        loads[-1].start()
    barrier = pltpu.get_barrier_semaphore()
    greeted = [sibling, across] + wav_peer
    for p in greeted:
        pl.semaphore_signal(barrier, inc=1, device_id=p, device_id_type=pl.DeviceIdType.MESH)
    pl.semaphore_wait(barrier, len(greeted))

    def remote(src, dst, ss, rs, device):
        return pltpu.make_async_remote_copy(
            src_ref=src, dst_ref=dst, send_sem=ss, recv_sem=rs,
            device_id=device, device_id_type=pl.DeviceIdType.MESH,
        )

    def part_cols(c):
        return pl.ds(0, SIDE + ac) if c == 0 else pl.ds(SIDE + c * ac, ac)

    def core_sum(s):
        return remote(ipart.at[s], crecv.at[s], cs_s.at[s], cs_r.at[s], sibling)

    def x_sum(s, slot):
        return remote(xsend.at[s], xrecv.at[slot, s], xx_s.at[slot, s], xx_r.at[slot, s], across)

    def core_share(s):
        return remote(masked.at[s, 0], masked.at[s, 1], cg_s.at[s], cg_r.at[s], sibling)

    def to_owner(s, c, o):
        k = lax.rem(wav - owners[o] + n - 1 + n, n)
        return remote(
            wpart.at[s, o, :, part_cols(c)],
            wrecv.at[s, k, :, part_cols(c)],
            ws_s.at[s, c, o],
            ws_r.at[s, c, k],
            {"wave": owners[o]},
        )

    def at_owner(s, c, k):
        return remote(
            wpart.at[s, 0, :, part_cols(c)],
            wrecv.at[s, k, :, part_cols(c)],
            ws_s.at[s, c, 0],
            ws_r.at[s, c, k],
            wav_peer[0],
        )

    def from_owner(s, c, o, k):
        return remote(
            probe.at[s, o, :, part_cols(c)],
            probe.at[s, o, :, part_cols(c)],
            ag_s.at[s, c, k],
            ag_r.at[s, c, o],
            wav_peer[k],
        )

    def kappa_copy(s, k):
        return remote(
            kappas.at[wav, s], kappas.at[wav, s], fin_s.at[s, k], fin_r.at[s, k], wav_peer[k]
        )

    def out_copy(s):
        return remote(field.at[s], other.at[s], out_s.at[s], out_r.at[s], sibling)

    def row_sum(values):
        return jnp.sum(values, axis=1, keepdims=True)

    def pack(values):
        lane = lax.broadcasted_iota(jnp.int32, (values[0].shape[0], SIDE), 1)
        packed = jnp.zeros(lane.shape, f32)
        for at, value in enumerate(values):
            rest = value
            for piece in range(3):
                top = rest.astype(bf16).astype(f32)
                rest = rest - top
                packed = jnp.where(lane == 3 * at + piece, top, packed)
        return packed.astype(bf16)

    def unpack(block, at=0):
        wide = block.astype(f32)
        low = 3 * at
        return wide[:, low:low + 1] + wide[:, low + 1:low + 2] + wide[:, low + 2:low + 3]

    def spread(column):
        return jnp.broadcast_to(column, (column.shape[0], LANES))

    def dot(lhs, rhs):
        return jnp.dot(lhs, rhs, preferred_element_type=f32)

    def make_image(s, k):
        def arrive(c):
            @pl.when(k > 0)
            def _():
                for o in range(OWNERS):
                    @pl.when(wav != owners[o])
                    def _():
                        from_owner(s, c, o, 0).wait_recv()

        def scalars(c, lhs):
            cols = slice(c * ac, (c + 1) * ac)
            wide = lhs.astype(f32)
            scaled = regul_ref[:, cols] * wide
            along = direction[s, :, :, cols].reshape(m, ac)
            return [row_sum(wide * wide), row_sum(scaled * wide), row_sum(scaled * along)]

        sums = None
        for c in range(CHUNKS):
            arrive(c)
            lhs = probe[s, :, :, SIDE + c * ac:SIDE + (c + 1) * ac].reshape(m, ac)
            more = scalars(c, lhs)
            sums = more if sums is None else [x + y for x, y in zip(sums, more)]
            for side in (1, 0):
                part = dot(lhs, jact[side, c * ac:(c + 1) * ac, :])
                cols = slice(side * half, (side + 1) * half)
                if c:
                    part = acc[:, cols] + part
                if c < CHUNKS - 1:
                    acc[:, cols] = part
                elif side == 1:
                    ipart[s, :, 0:SIDE] = pack(sums)
                    ipart[s, :, SIDE:] = part.astype(bf16)
                    core_sum(s).start()
                else:
                    qown[s] = part
        step = unpack(probe[s, :, :, 0:SIDE].reshape(m, SIDE))
        field[s] = field[s] + step * img[s]
        step = step.reshape(OWNERS, mo, 1)
        change[s] = change[s] + step * direction[s]

    def join_cores(s, k):
        core_sum(s).wait()
        both = [unpack(ipart[s, :, 0:SIDE], at) + unpack(crecv[s, :, 0:SIDE], at) for at in range(3)]
        xsend[s, :, 0:SIDE] = pack(both)
        xsend[s, :, SIDE:] = (qown[s] + crecv[s, :, SIDE:].astype(f32)).astype(bf16)
        x_sum(s, lax.rem(k, 2)).start()

    def take_image(s, k):
        slot = lax.rem(k, 2)
        x_sum(s, slot).wait()
        norm, aa, bb = [
            unpack(xsend[s, :, 0:SIDE], at) + unpack(xrecv[slot, s, :, 0:SIDE], at) for at in range(3)
        ]
        norm_before = gamma[s].reshape(m, LANES)[:, 0:1]
        rho_before = rho[s].reshape(m, LANES)[:, 0:1]
        ratio = norm / (norm_before + epsilon)
        ratio = jnp.where(lax.rem(k, CG) == 1, 0.0, ratio)
        ratio = jnp.where(k == 0, 1.0, ratio)
        rho_now = jnp.maximum(aa + 2.0 * ratio * bb + ratio * ratio * rho_before, 0.0)
        gamma[s] = spread(norm).reshape(OWNERS, mo, LANES)
        rho[s] = spread(rho_now).reshape(OWNERS, mo, LANES)
        now = xsend[s, :, SIDE:].astype(f32) + xrecv[slot, s, :, SIDE:].astype(f32) + ratio * img[s]
        img[s] = now
        kept = (weight_ref[...] * now).astype(bf16)
        masked[s, 0, :, SIDE:] = kept
        wide = kept.astype(f32)
        masked[s, 0, :, 0:SIDE] = pack([row_sum(wide * wide)])
        core_share(s).start()
        fresh = jnp.where(k == 0, 0.0, 1.0)
        direction[s] = (
            fresh * probe[s, :, :, SIDE:].astype(f32) + ratio.reshape(OWNERS, mo, 1) * direction[s]
        )

        @pl.when(k > 0)
        def _():
            for c in range(CHUNKS):
                for o in range(OWNERS):
                    @pl.when(wav != owners[o])
                    def _():
                        to_owner(s, c, o).wait_send()

            @pl.when(is_owner)
            def _():
                for c in range(CHUNKS):
                    for p in peers:
                        from_owner(s, c, mine, p).wait_send()

    def wave_kappa(s):
        return unpack(masked[s, 0, :, 0:SIDE]) + unpack(masked[s, 1, :, 0:SIDE])

    def make_back(s):
        lhs = masked[s, 0, :, SIDE:]
        for c in range(CHUNKS):
            cols = slice(c * ac, (c + 1) * ac)
            acc[:, cols] = dot(lhs, jac[0, :, cols])
        core_share(s).wait()
        wpart[s, :, :, 0:SIDE] = pack([wave_kappa(s)]).reshape(OWNERS, mo, SIDE)
        lhs = masked[s, 1, :, SIDE:]
        for c in range(CHUNKS):
            cols = slice(c * ac, (c + 1) * ac)
            part = acc[:, cols] + dot(lhs, jac[1, :, cols])
            wpart[s, :, :, SIDE + c * ac:SIDE + (c + 1) * ac] = part.astype(bf16).reshape(OWNERS, mo, ac)
            for o in range(OWNERS):
                @pl.when(wav != owners[o])
                def _():
                    to_owner(s, c, o).start()

    def update(s, k):
        @pl.when(is_owner)
        def _():
            again = jnp.where(k == CG, 1.0, 0.0)
            for c in range(CHUNKS):
                for p in peers:
                    at_owner(s, c, p).wait_recv()
                if c == 0:
                    kappa = unpack(wpart[s, mine, :, 0:SIDE])
                    for p in peers:
                        kappa = kappa + unpack(wrecv[s, p, :, 0:SIDE])
                    norm, rho_now = gamma[s, mine][:, 0:1], rho[s, mine][:, 0:1]
                    step = norm / (kappa + rho_now + epsilon)
                    step = jnp.where(k == 0, 1.0, step)
                    probe[s, mine, :, 0:SIDE] = pack([step])
                cols = slice(c * ac, (c + 1) * ac)
                wide = slice(SIDE + c * ac, SIDE + (c + 1) * ac)
                total = wpart[s, mine, :, wide].astype(f32)
                for p in peers:
                    total = total + wrecv[s, p, :, wide].astype(f32)
                along = direction[s, mine, :, cols]
                weight = regul_ref[:, cols]
                after = residual[s, :, cols] - step * (total + weight * along)
                after = after + again * (weight * (change[s, mine, :, cols] + step * along))
                residual[s, :, cols] = after
                probe[s, mine, :, wide] = after.astype(bf16)
                for p in peers:
                    from_owner(s, c, mine, p).start()

    def send_kappa(s):
        core_share(s).wait()
        kappas[wav, s] = spread(wave_kappa(s))
        for p in peers:
            kappa_copy(s, p).start()

    def finish(s):
        for p in peers:
            kappa_copy(s, p).wait()
        kappa = kappas[0, s]
        for w in range(1, n):
            kappa = kappa + kappas[w, s]
        step = gamma[s].reshape(m, LANES) / (kappa + rho[s].reshape(m, LANES) + epsilon)
        step = step[:, 0:1]
        field[s] = field[s] + step * img[s]
        out_copy(s).start()
        rows = slice(s * m, (s + 1) * m)
        moved = change[s] + step.reshape(OWNERS, mo, 1) * direction[s]
        cmd_ref[rows, :] = start_ref[rows, :] + moved.reshape(m, acts)
        out_ref[rows, pl.ds(pl.multiple_of(core * half, half), half)] = field[s]

    def finish_other(s):
        out_copy(s).wait()
        rows = slice(s * m, (s + 1) * m)
        out_ref[rows, pl.ds(pl.multiple_of((1 - core) * half, half), half)] = other[s]

    for s in range(STREAMS):
        probe[s, :, :, 0:SIDE] = jnp.zeros((OWNERS, mo, SIDE), bf16)
        probe[s, :, :, SIDE:] = start_ref[s * m:(s + 1) * m, :].astype(bf16).reshape(OWNERS, mo, acts)
        img[s] = base_ref[s * m:(s + 1) * m, :]
    for ref in (field, direction, change, residual, gamma, rho):
        ref[...] = jnp.zeros_like(ref)
    block = 256
    for side in (1, 0):
        loads[side].wait()

        def turn(i, carry):
            at = pl.multiple_of(i * block, block)
            jact[side, :, pl.ds(at, block)] = jac[side, pl.ds(at, block), :].T
            return carry

        lax.fori_loop(0, half // block, turn, 0)

    def turn_half(t, carry):
        here, there = lax.rem(t + 1, 2), lax.rem(t, 2)
        k_here = (t + 1) // 2 - 1
        k_there = t // 2

        @pl.when(t >= 1)
        def _():
            join_cores(here, k_here)

        @pl.when(jnp.logical_and(t >= 2, t <= 2 * last + 1))
        def _():
            update(there, k_there - 1)

        @pl.when(t >= 1)
        def _():
            take_image(here, k_here)

        @pl.when(jnp.logical_and(t >= 1, t <= 2 * last))
        def _():
            make_back(here)

        @pl.when(t > 2 * last)
        def _():
            send_kappa(here)

        @pl.when(t <= 2 * last + 1)
        def _():
            make_image(there, k_there)

        return carry

    lax.fori_loop(0, 2 * last + 3, turn_half, 0)
    for s in range(STREAMS):
        finish(s)
    for s in range(STREAMS):
        finish_other(s)


def kernel_shards(nominal_field, sensitivity, aberrations, jacobian, tile_mask, regul, initial_commands):
    f32, bf16 = jnp.float32, jnp.bfloat16
    components, pixels, acts = jacobian.shape[1:]
    rows = components * pixels
    half = pixels
    reals = initial_commands.shape[0]
    n = lax.axis_size("section")
    m = reals // STREAMS
    mo = m // OWNERS
    tile_count = tile_mask.shape[1]
    weight = jnp.broadcast_to(
        tile_mask[0].astype(f32)[:, None], (tile_count, pixels // tile_count)
    ).reshape(1, pixels)
    core = lax.rem(lax.axis_index("section"), 2)
    own = lax.dynamic_index_in_dim(sensitivity[0], core, 1, keepdims=False)
    base = lax.dynamic_index_in_dim(nominal_field[0], core, 0) + jnp.dot(
        aberrations, own, preferred_element_type=f32
    )
    vmem = pl.BlockSpec(memory_space=pltpu.VMEM)
    dma = pltpu.SemaphoreType.DMA
    commands, field = pl.pallas_call(
        functools.partial(control_kernel, n),
        out_shape=(
            jax.ShapeDtypeStruct((reals, acts), f32),
            jax.ShapeDtypeStruct((reals, rows), f32),
        ),
        in_specs=[pl.BlockSpec(memory_space=pl.ANY), vmem, vmem, vmem, vmem],
        out_specs=(vmem, vmem),
        scratch_shapes=[
            pltpu.VMEM((2, half, acts), bf16),
            pltpu.VMEM((2, acts, half), bf16),
            pltpu.VMEM((STREAMS, OWNERS, mo, SIDE + acts), bf16),
            pltpu.VMEM((STREAMS, OWNERS, mo, SIDE + acts), bf16),
            pltpu.VMEM((STREAMS, n - 1, mo, SIDE + acts), bf16),
            pltpu.VMEM((STREAMS, m, SIDE + half), bf16),
            pltpu.VMEM((STREAMS, m, SIDE + half), bf16),
            pltpu.VMEM((STREAMS, m, SIDE + half), bf16),
            pltpu.VMEM((2, STREAMS, m, SIDE + half), bf16),
            pltpu.VMEM((STREAMS, 2, m, SIDE + half), bf16),
            pltpu.VMEM((STREAMS, m, half), f32),
            pltpu.VMEM((STREAMS, m, half), f32),
            pltpu.VMEM((STREAMS, m, half), f32),
            pltpu.VMEM((STREAMS, OWNERS, mo, acts), f32),
            pltpu.VMEM((STREAMS, OWNERS, mo, acts), f32),
            pltpu.VMEM((STREAMS, mo, acts), f32),
            pltpu.VMEM((m, max(2 * half, acts)), f32),
            pltpu.VMEM((STREAMS, OWNERS, mo, LANES), f32),
            pltpu.VMEM((STREAMS, OWNERS, mo, LANES), f32),
            pltpu.VMEM((n, STREAMS, m, LANES), f32),
            pltpu.VMEM((STREAMS, m, half), f32),
            dma((2,)),
            dma((STREAMS,)),
            dma((STREAMS,)),
            dma((2, STREAMS)),
            dma((2, STREAMS)),
            dma((STREAMS,)),
            dma((STREAMS,)),
            dma((STREAMS, CHUNKS, OWNERS)),
            dma((STREAMS, CHUNKS, n - 1)),
            dma((STREAMS, CHUNKS, n - 1)),
            dma((STREAMS, CHUNKS, OWNERS)),
            dma((STREAMS, n - 1)),
            dma((STREAMS, n - 1)),
            dma((STREAMS,)),
            dma((STREAMS,)),
        ],
        compiler_params=pltpu.CompilerParams(
            collective_id=0, has_side_effects=True, vmem_limit_bytes=44 * 1024 * 1024
        ),
        name="control_loop",
    )(
        jacobian.reshape(rows, acts),
        base,
        initial_commands,
        regul[None, :],
        weight,
    )
    return commands, field.reshape(reals, 1, components, pixels)


def solution(mesh):
    placed = (
        P("wave", None, None),
        P("wave", None, None, None),
        P("groups", None),
        P("wave", None, None, "section"),
        P("wave", None),
        P("section"),
        P("groups", "section"),
    )

    def choose(*args):
        n, waves = mesh.shape["section"], mesh.shape["wave"]
        reals = args[6].shape[0]
        acts = args[3].shape[3]
        pixels = args[3].shape[2]
        fits = (
            n == 4
            and waves == 4
            and args[3].shape[1] == 2
            and reals % (16 * STREAMS * OWNERS) == 0
            and acts % (LANES * CHUNKS) == 0
            and pixels % (2 * LANES) == 0
            and 2 * pixels * acts <= 2048 * 2048
            and reals <= 64
        )
        return (kernel_shards if fits else general_shards)(*args)

    return jax.shard_map(
        choose,
        mesh=mesh,
        in_specs=placed,
        out_specs=(P("groups", "section"), P("groups", "wave", None, None)),
        check_vma=False,
    )
```

```python
import functools

import jax
import jax.numpy as jnp
from jax import lax
from jax.experimental import pallas as pl
from jax.experimental.pallas import tpu as pltpu
from jax.sharding import PartitionSpec as P

ITERS = 2
CG = 5
LANES = 128
CHUNKS = 2
STREAMS = 2
OWNERS = 2
SIDE = 128
BLOCKS = 4
PAD = 128

epsilon = 1e-06


def to_section_image(command_bf, jac_block):
    partial_value = lax.dot_general(
        command_bf, jac_block, (((1,), (1,)), ((), ())), preferred_element_type=jnp.float32
    )
    return lax.psum_scatter(
        partial_value.astype(jnp.bfloat16), "section", scatter_dimension=1, tiled=True
    ).astype(jnp.float32)


def back_of(masked_share, jac_block):
    masked_bf = lax.all_gather(masked_share, "section", axis=1, tiled=True)
    partial_value = jnp.dot(masked_bf, jac_block, preferred_element_type=jnp.float32)
    owned = lax.psum_scatter(
        partial_value.astype(jnp.bfloat16), "wave", scatter_dimension=1, tiled=True
    ).astype(jnp.float32)
    return lax.all_gather(owned, "wave", axis=1, tiled=True)


def reduce_scalars(values):
    return lax.psum(values, "section")


def general_shards(nominal_field, sensitivity, aberrations, jacobian, tile_mask, regul, initial_commands):
    components = jacobian.shape[1]
    pixels = jacobian.shape[2]
    block_width = jacobian.shape[3]
    row_count = components * pixels
    share_rows = row_count // lax.axis_size("section")
    row_start = lax.axis_index("section") * share_rows
    jac_block = jacobian.reshape(row_count, block_width)
    tile_count = tile_mask.shape[1]
    weight_full = jnp.broadcast_to(
        tile_mask[0].astype(jnp.float32)[None, :, None],
        (components, tile_count, pixels // tile_count),
    ).reshape(1, row_count)
    weight = lax.dynamic_slice_in_dim(weight_full, row_start, share_rows, 1)
    mode_count = sensitivity.shape[1]
    sens_share = lax.dynamic_slice_in_dim(
        sensitivity.reshape(mode_count, row_count), row_start, share_rows, 1
    )
    nominal_share = lax.dynamic_slice_in_dim(
        nominal_field.reshape(1, row_count), row_start, share_rows, 1
    )
    field_now = nominal_share + jnp.dot(aberrations, sens_share, preferred_element_type=jnp.float32)
    commands = initial_commands
    field_now = field_now + to_section_image(commands.astype(jnp.bfloat16), jac_block)
    for iteration in range(ITERS):
        residual = -back_of((weight * field_now).astype(jnp.bfloat16), jac_block)
        direction = residual
        change = jnp.zeros_like(residual)
        field_step = jnp.zeros_like(field_now)
        norm_now = reduce_scalars(jnp.sum(residual * residual, axis=1))
        for inner_step in range(CG):
            image_now = to_section_image(direction.astype(jnp.bfloat16), jac_block)
            applied = (
                back_of((weight * image_now).astype(jnp.bfloat16), jac_block)
                + regul[None, :] * direction
            )
            curvature = reduce_scalars(jnp.sum(direction * applied, axis=1))
            step_len = norm_now / (curvature + epsilon)
            residual = residual - step_len[:, None] * applied
            norm_next = reduce_scalars(jnp.sum(residual * residual, axis=1))
            change = change + step_len[:, None] * direction
            field_step = field_step + step_len[:, None] * image_now
            direction = residual + (norm_next / (norm_now + epsilon))[:, None] * direction
            norm_now = norm_next
        commands = commands + change
        field_now = field_now + field_step
    whole_field = lax.all_gather(
        field_now.astype(jnp.bfloat16), "section", axis=1, tiled=True
    ).astype(field_now.dtype)
    return (commands, whole_field.reshape(whole_field.shape[0], 1, components, pixels))


def control_kernel(
    n,
    jac_hbm,
    base_ref,
    start_ref,
    regul_ref,
    weight_ref,
    cmd_ref,
    out_ref,
    jac,
    jact,
    probe,
    wpart,
    wrecv,
    ipart,
    crecv,
    xsend,
    xrecv,
    masked,
    img,
    field,
    qown,
    direction,
    change,
    residual,
    acc,
    gamma,
    rho,
    kappas,
    other,
    lost,
    owed,
    opart,
    orecv,
    jac_sem,
    cs_s,
    cs_r,
    xx_s,
    xx_r,
    cg_s,
    cg_r,
    ws_s,
    ws_r,
    ag_s,
    ag_r,
    fin_s,
    fin_r,
    out_s,
    out_r,
    ow_s,
    ow_r,
):
    f32, bf16 = jnp.float32, jnp.bfloat16
    half, acts = jac.shape[1:]
    mo = probe.shape[2]
    m = OWNERS * mo
    ac = acts // CHUNKS
    last = ITERS * CG
    sec, wav = lax.axis_index("section"), lax.axis_index("wave")
    core = lax.rem(sec, 2)
    sibling = {"section": sec + 1 - 2 * core}
    across = {"section": lax.rem(sec + 2, n)}
    first_owner = n // 2 - 1
    owners = [first_owner + o for o in range(OWNERS)]
    is_owner = jnp.logical_and(wav >= owners[0], wav <= owners[-1])
    far = jnp.where(wav <= first_owner, 1, 0)
    mine = jnp.clip(wav - first_owner, 0, OWNERS - 1)
    peers = range(n - 1)
    wav_peer = [{"wave": lax.rem(wav + k + 1, n)} for k in peers]

    block = half // BLOCKS

    def load(side, i):
        at = pl.multiple_of((core if side == 0 else 1 - core) * half + i * block, block)
        return pltpu.make_async_copy(
            jac_hbm.at[pl.ds(at, block)], jac.at[side, pl.ds(i * block, block)], jac_sem.at[side, i]
        )

    for side in (1, 0):
        for i in range(BLOCKS):
            load(side, i).start()
    barrier = pltpu.get_barrier_semaphore()
    greeted = [sibling, across] + wav_peer
    for p in greeted:
        pl.semaphore_signal(barrier, inc=1, device_id=p, device_id_type=pl.DeviceIdType.MESH)
    pl.semaphore_wait(barrier, len(greeted))

    def remote(src, dst, ss, rs, device):
        return pltpu.make_async_remote_copy(
            src_ref=src, dst_ref=dst, send_sem=ss, recv_sem=rs,
            device_id=device, device_id_type=pl.DeviceIdType.MESH,
        )

    def part_cols(c):
        return pl.ds(0, SIDE + ac) if c == 0 else pl.ds(SIDE + c * ac, ac)

    def core_sum(s):
        return remote(ipart.at[s], crecv.at[s], cs_s.at[s], cs_r.at[s], sibling)

    def x_sum(s, slot):
        return remote(xsend.at[s], xrecv.at[slot, s], xx_s.at[slot, s], xx_r.at[slot, s], across)

    def core_share(s):
        return remote(masked.at[s, 0], masked.at[s, 1], cg_s.at[s], cg_r.at[s], sibling)

    def to_owner(s, c, o):
        owner = first_owner + o
        k = lax.rem(wav - owner + n - 1 + n, n)
        return remote(
            wpart.at[s, o, :, part_cols(c)],
            wrecv.at[s, k, :, part_cols(c)],
            ws_s.at[s, c, o],
            ws_r.at[s, c, k],
            {"wave": owner},
        )

    def owed_copy(s, o):
        owner = first_owner + o
        k = lax.rem(wav - owner + n - 1 + n, n)
        return remote(
            opart.at[s, o], orecv.at[s, k], ow_s.at[s, o], ow_r.at[s, k], {"wave": owner}
        )

    def owed_at(s, k):
        return remote(opart.at[s, 0], orecv.at[s, k], ow_s.at[s, 0], ow_r.at[s, k], wav_peer[0])

    def at_owner(s, c, k):
        return remote(
            wpart.at[s, 0, :, part_cols(c)],
            wrecv.at[s, k, :, part_cols(c)],
            ws_s.at[s, c, 0],
            ws_r.at[s, c, k],
            wav_peer[0],
        )

    def from_owner(s, c, o, k):
        return remote(
            probe.at[s, o, :, part_cols(c)],
            probe.at[s, o, :, part_cols(c)],
            ag_s.at[s, c, k],
            ag_r.at[s, c, o],
            wav_peer[k],
        )

    def kappa_copy(s, k):
        return remote(
            kappas.at[wav, s], kappas.at[wav, s], fin_s.at[s, k], fin_r.at[s, k], wav_peer[k]
        )

    def out_copy(s):
        return remote(field.at[s], other.at[s], out_s.at[s], out_r.at[s], sibling)

    def row_sum(values):
        return jnp.sum(values, axis=1, keepdims=True)

    def pack(values):
        lane = lax.broadcasted_iota(jnp.int32, (values[0].shape[0], SIDE), 1)
        packed = jnp.zeros(lane.shape, f32)
        for at, value in enumerate(values):
            rest = value
            for piece in range(3):
                top = rest.astype(bf16).astype(f32)
                rest = rest - top
                packed = jnp.where(lane == 3 * at + piece, top, packed)
        return packed.astype(bf16)

    def beside(block, more):
        return block.astype(f32) + pltpu.roll(more.astype(f32), 16, 1)

    def pick(lanes, at):
        lane = lax.rem(lax.broadcasted_iota(jnp.int32, lanes.shape, 1), 16)
        return row_sum(jnp.where(jnp.logical_and(lane >= 3 * at, lane < 3 * at + 3), lanes, 0.0))

    def spread(column):
        return jnp.broadcast_to(column, (column.shape[0], LANES))

    def dot(lhs, rhs):
        padded = jnp.concatenate([lhs, jnp.zeros((PAD - m, lhs.shape[1]), bf16)], axis=0)
        return jnp.dot(padded, rhs, preferred_element_type=f32)[:m]

    def make_image(s, k):
        def arrive(c):
            @pl.when(k > 0)
            def _():
                for o in range(OWNERS):
                    @pl.when(wav != owners[o])
                    def _():
                        from_owner(s, c, o, 0).wait_recv()

        def scalars(c, lhs):
            cols = slice(c * ac, (c + 1) * ac)
            wide = lhs.astype(f32)
            scaled = regul_ref[:, cols] * wide
            along = direction[s, :, :, cols].reshape(m, ac)
            return [row_sum(wide * wide), row_sum(scaled * wide), row_sum(scaled * along)]

        sums = None
        for c in range(CHUNKS):
            arrive(c)
            lhs = probe[s, :, :, SIDE + c * ac:SIDE + (c + 1) * ac].reshape(m, ac)
            more = scalars(c, lhs)
            sums = more if sums is None else [x + y for x, y in zip(sums, more)]
            for side in (1, 0):
                part = dot(lhs, jact[side, c * ac:(c + 1) * ac, :])
                cols = slice(side * half, (side + 1) * half)
                if c:
                    part = acc[:, cols] + part
                if c < CHUNKS - 1:
                    acc[:, cols] = part
                elif side == 1:
                    ipart[s, :, 0:SIDE] = pack(sums)
                    ipart[s, :, SIDE:] = part.astype(bf16)
                    core_sum(s).start()
                else:
                    qown[s] = part
        step = row_sum(probe[s, :, :, 0:SIDE].reshape(m, SIDE).astype(f32))
        field[s] = field[s] + step * img[s]
        step = step.reshape(OWNERS, mo, 1)
        change[s] = change[s] + step * direction[s]
        owed[s] = owed[s] + step * lost[s]

    def settle(s):
        for p in peers:
            owed_at(s, p).wait_recv()
        total = opart[s, mine].astype(f32)
        for p in peers:
            total = total + orecv[s, p].astype(f32)
        residual[s] = residual[s] - total

    def join_cores(s, k):
        core_sum(s).wait()
        xsend[s, :, 0:SIDE] = beside(ipart[s, :, 0:SIDE], crecv[s, :, 0:SIDE]).astype(bf16)
        xsend[s, :, SIDE:] = (qown[s] + crecv[s, :, SIDE:].astype(f32)).astype(bf16)
        x_sum(s, lax.rem(k, 2)).start()

        @pl.when(k == CG)
        def _():
            opart[s] = owed[s].astype(bf16)
            owed_copy(s, far).start()

            @pl.when(jnp.logical_not(is_owner))
            def _():
                owed_copy(s, 1 - far).start()

    def take_image(s, k):
        slot = lax.rem(k, 2)
        x_sum(s, slot).wait()
        lanes = xsend[s, :, 0:SIDE].astype(f32) + xrecv[slot, s, :, 0:SIDE].astype(f32)
        norm, aa, bb = [pick(lanes, at) for at in range(3)]
        norm_before = gamma[s].reshape(m, LANES)[:, 0:1]
        rho_before = rho[s].reshape(m, LANES)[:, 0:1]
        ratio = norm / (norm_before + epsilon)
        ratio = jnp.where(lax.rem(k, CG) == 1, 0.0, ratio)
        ratio = jnp.where(k == 0, 1.0, ratio)
        rho_now = jnp.maximum(aa + 2.0 * ratio * bb + ratio * ratio * rho_before, 0.0)
        gamma[s] = spread(norm).reshape(OWNERS, mo, LANES)
        rho[s] = spread(rho_now).reshape(OWNERS, mo, LANES)
        now = xsend[s, :, SIDE:].astype(f32) + xrecv[slot, s, :, SIDE:].astype(f32) + ratio * img[s]
        img[s] = now
        kept = (weight_ref[...] * now).astype(bf16)
        masked[s, 0] = kept
        core_share(s).start()
        fresh = jnp.where(k == 0, 0.0, 1.0)
        direction[s] = (
            fresh * probe[s, :, :, SIDE:].astype(f32) + ratio.reshape(OWNERS, mo, 1) * direction[s]
        )

        @pl.when(k > 0)
        def _():
            for c in range(CHUNKS):
                to_owner(s, c, far).wait_send()

                @pl.when(jnp.logical_not(is_owner))
                def _():
                    to_owner(s, c, 1 - far).wait_send()

            @pl.when(is_owner)
            def _():
                for c in range(CHUNKS):
                    for p in peers:
                        from_owner(s, c, mine, p).wait_send()

            @pl.when(k == CG + 1)
            def _():
                owed_copy(s, far).wait_send()

                @pl.when(jnp.logical_not(is_owner))
                def _():
                    owed_copy(s, 1 - far).wait_send()

    def square(s, side):
        wide = masked[s, side].astype(f32)
        return row_sum(wide * wide)

    def make_back(s):
        lhs = masked[s, 0]
        for c in range(CHUNKS):
            cols = slice(c * ac, (c + 1) * ac)
            acc[:, cols] = dot(lhs, jac[0, :, cols])
        kappa = square(s, 0)
        core_share(s).wait()
        kappa = pack([kappa + square(s, 1)])
        wpart[s, :, :, 0:SIDE] = kappa.reshape(OWNERS, mo, SIDE)
        lhs = masked[s, 1]
        for c in range(CHUNKS):
            cols = slice(c * ac, (c + 1) * ac)
            part = acc[:, cols] + dot(lhs, jac[1, :, cols])
            sent = part.astype(bf16)
            wpart[s, :, :, SIDE + c * ac:SIDE + (c + 1) * ac] = sent.reshape(OWNERS, mo, ac)
            to_owner(s, c, far).start()

            @pl.when(jnp.logical_not(is_owner))
            def _():
                to_owner(s, c, 1 - far).start()

            lost[s, :, :, cols] = (part - sent.astype(f32)).reshape(OWNERS, mo, ac)

    def update(s, k):
        @pl.when(is_owner)
        def _():
            again = jnp.where(k == CG, 1.0, 0.0)

            @pl.when(k == CG)
            def _():
                settle(s)

            for c in range(CHUNKS):
                for p in peers:
                    at_owner(s, c, p).wait_recv()
                if c == 0:
                    kappa = wpart[s, mine, :, 0:SIDE].astype(f32)
                    for p in peers:
                        kappa = kappa + wrecv[s, p, :, 0:SIDE].astype(f32)
                    kappa = row_sum(kappa)
                    norm, rho_now = gamma[s, mine][:, 0:1], rho[s, mine][:, 0:1]
                    step = norm / (kappa + rho_now + epsilon)
                    step = jnp.where(k == 0, 1.0, step)
                    probe[s, mine, :, 0:SIDE] = pack([step])
                cols = slice(c * ac, (c + 1) * ac)
                wide = slice(SIDE + c * ac, SIDE + (c + 1) * ac)
                total = wpart[s, mine, :, wide].astype(f32)
                for p in peers:
                    total = total + wrecv[s, p, :, wide].astype(f32)
                along = direction[s, mine, :, cols]
                weight = regul_ref[:, cols]
                after = residual[s, :, cols] - step * (total + weight * along)
                after = after + again * (weight * (change[s, mine, :, cols] + step * along))
                residual[s, :, cols] = after
                probe[s, mine, :, wide] = after.astype(bf16)
                for p in (1, 0, 2):
                    from_owner(s, c, mine, p).start()

    def send_kappa(s):
        core_share(s).wait()
        kappas[wav, s] = spread(square(s, 0) + square(s, 1))
        for p in peers:
            kappa_copy(s, p).start()

    def finish(s):
        for p in peers:
            kappa_copy(s, p).wait()
        kappa = kappas[0, s]
        for w in range(1, n):
            kappa = kappa + kappas[w, s]
        kappa = kappa[:, 0:1]
        step = gamma[s].reshape(m, LANES)[:, 0:1]
        step = step / (kappa + rho[s].reshape(m, LANES)[:, 0:1] + epsilon)
        field[s] = field[s] + step * img[s]
        out_copy(s).start()
        rows = slice(s * m, (s + 1) * m)
        moved = change[s] + step.reshape(OWNERS, mo, 1) * direction[s]
        cmd_ref[rows, :] = start_ref[rows, :] + moved.reshape(m, acts)
        out_ref[rows, pl.ds(pl.multiple_of(core * half, half), half)] = field[s]

    def finish_other(s):
        out_copy(s).wait()
        rows = slice(s * m, (s + 1) * m)
        out_ref[rows, pl.ds(pl.multiple_of((1 - core) * half, half), half)] = other[s]

    for s in range(STREAMS):
        probe[s, :, :, 0:SIDE] = jnp.zeros((OWNERS, mo, SIDE), bf16)
        probe[s, :, :, SIDE:] = start_ref[s * m:(s + 1) * m, :].astype(bf16).reshape(OWNERS, mo, acts)
        img[s] = base_ref[s * m:(s + 1) * m, :]
    for ref in (field, direction, change, residual, gamma, rho, lost, owed):
        ref[...] = jnp.zeros_like(ref)
    for side in (1, 0):

        def turn(i, carry):
            load(side, i).wait()
            at = pl.multiple_of(i * block, block)
            jact[side, :, pl.ds(at, block)] = jac[side, pl.ds(at, block), :].T
            return carry

        lax.fori_loop(0, BLOCKS, turn, 0)

    def turn_half(t, carry):
        here, there = lax.rem(t + 1, 2), lax.rem(t, 2)
        k_here = (t + 1) // 2 - 1
        k_there = t // 2

        @pl.when(t >= 1)
        def _():
            join_cores(here, k_here)

        @pl.when(jnp.logical_and(t >= 2, t <= 2 * last + 1))
        def _():
            update(there, k_there - 1)

        @pl.when(t >= 1)
        def _():
            take_image(here, k_here)

        @pl.when(jnp.logical_and(t >= 1, t <= 2 * last))
        def _():
            make_back(here)

        @pl.when(t > 2 * last)
        def _():
            send_kappa(here)

        @pl.when(t <= 2 * last + 1)
        def _():
            make_image(there, k_there)

        return carry

    lax.fori_loop(0, 2 * last + 3, turn_half, 0)
    for s in range(STREAMS):
        finish(s)
    for s in range(STREAMS):
        finish_other(s)


def kernel_shards(nominal_field, sensitivity, aberrations, jacobian, tile_mask, regul, initial_commands):
    f32, bf16 = jnp.float32, jnp.bfloat16
    components, pixels, acts = jacobian.shape[1:]
    rows = components * pixels
    half = pixels
    reals = initial_commands.shape[0]
    n = lax.axis_size("section")
    m = reals // STREAMS
    mo = m // OWNERS
    tile_count = tile_mask.shape[1]
    weight = jnp.broadcast_to(
        tile_mask[0].astype(f32)[:, None], (tile_count, pixels // tile_count)
    ).reshape(1, pixels)
    core = lax.rem(lax.axis_index("section"), 2)
    own = lax.dynamic_index_in_dim(sensitivity[0], core, 1, keepdims=False)
    base = lax.dynamic_index_in_dim(nominal_field[0], core, 0) + jnp.dot(
        aberrations, own, preferred_element_type=f32
    )
    vmem = pl.BlockSpec(memory_space=pltpu.VMEM)
    dma = pltpu.SemaphoreType.DMA
    commands, field = pl.pallas_call(
        functools.partial(control_kernel, n),
        out_shape=(
            jax.ShapeDtypeStruct((reals, acts), f32),
            jax.ShapeDtypeStruct((reals, rows), f32),
        ),
        in_specs=[pl.BlockSpec(memory_space=pl.ANY), vmem, vmem, vmem, vmem],
        out_specs=(vmem, vmem),
        scratch_shapes=[
            pltpu.VMEM((2, half, acts), bf16),
            pltpu.VMEM((2, acts, half), bf16),
            pltpu.VMEM((STREAMS, OWNERS, mo, SIDE + acts), bf16),
            pltpu.VMEM((STREAMS, OWNERS, mo, SIDE + acts), bf16),
            pltpu.VMEM((STREAMS, n - 1, mo, SIDE + acts), bf16),
            pltpu.VMEM((STREAMS, m, SIDE + half), bf16),
            pltpu.VMEM((STREAMS, m, SIDE + half), bf16),
            pltpu.VMEM((STREAMS, m, SIDE + half), bf16),
            pltpu.VMEM((2, STREAMS, m, SIDE + half), bf16),
            pltpu.VMEM((STREAMS, 2, m, half), bf16),
            pltpu.VMEM((STREAMS, m, half), f32),
            pltpu.VMEM((STREAMS, m, half), f32),
            pltpu.VMEM((STREAMS, m, half), f32),
            pltpu.VMEM((STREAMS, OWNERS, mo, acts), f32),
            pltpu.VMEM((STREAMS, OWNERS, mo, acts), f32),
            pltpu.VMEM((STREAMS, mo, acts), f32),
            pltpu.VMEM((m, max(2 * half, acts)), f32),
            pltpu.VMEM((STREAMS, OWNERS, mo, LANES), f32),
            pltpu.VMEM((STREAMS, OWNERS, mo, LANES), f32),
            pltpu.VMEM((n, STREAMS, m, LANES), f32),
            pltpu.VMEM((STREAMS, m, half), f32),
            pltpu.VMEM((STREAMS, OWNERS, mo, acts), f32),
            pltpu.VMEM((STREAMS, OWNERS, mo, acts), f32),
            pltpu.VMEM((STREAMS, OWNERS, mo, acts), bf16),
            pltpu.VMEM((STREAMS, n - 1, mo, acts), bf16),
            dma((2, BLOCKS)),
            dma((STREAMS,)),
            dma((STREAMS,)),
            dma((2, STREAMS)),
            dma((2, STREAMS)),
            dma((STREAMS,)),
            dma((STREAMS,)),
            dma((STREAMS, CHUNKS, OWNERS)),
            dma((STREAMS, CHUNKS, n - 1)),
            dma((STREAMS, CHUNKS, n - 1)),
            dma((STREAMS, CHUNKS, OWNERS)),
            dma((STREAMS, n - 1)),
            dma((STREAMS, n - 1)),
            dma((STREAMS,)),
            dma((STREAMS,)),
            dma((STREAMS, OWNERS)),
            dma((STREAMS, n - 1)),
        ],
        compiler_params=pltpu.CompilerParams(
            collective_id=0, has_side_effects=True, vmem_limit_bytes=56 * 1024 * 1024
        ),
        name="control_loop",
    )(
        jacobian.reshape(rows, acts),
        base,
        initial_commands,
        regul[None, :],
        weight,
    )
    return commands, field.reshape(reals, 1, components, pixels)


def solution(mesh):
    placed = (
        P("wave", None, None),
        P("wave", None, None, None),
        P("groups", None),
        P("wave", None, None, "section"),
        P("wave", None),
        P("section"),
        P("groups", "section"),
    )

    def choose(*args):
        n, waves = mesh.shape["section"], mesh.shape["wave"]
        reals = args[6].shape[0]
        acts = args[3].shape[3]
        pixels = args[3].shape[2]
        fits = (
            n == 4
            and waves == 4
            and args[3].shape[1] == 2
            and reals % (16 * STREAMS * OWNERS) == 0
            and acts % (LANES * CHUNKS) == 0
            and pixels % (2 * LANES) == 0
            and 2 * pixels * acts <= 2048 * 2048
            and reals <= 64
        )
        return (kernel_shards if fits else general_shards)(*args)

    return jax.shard_map(
        choose,
        mesh=mesh,
        in_specs=placed,
        out_specs=(P("groups", "section"), P("groups", "wave", None, None)),
        check_vma=False,
    )
```

```python
import functools

import jax
import jax.numpy as jnp
from jax import lax
from jax.experimental import pallas as pl
from jax.experimental.pallas import tpu as pltpu
from jax.sharding import PartitionSpec as P

ITERS = 2
CG = 5
LANES = 128
CHUNKS = 2
STREAMS = 2
OWNERS = 2
SIDE = 128
BLOCKS = 4
PAD = 128

epsilon = 1e-06


def to_section_image(command_bf, jac_block):
    partial_value = lax.dot_general(
        command_bf, jac_block, (((1,), (1,)), ((), ())), preferred_element_type=jnp.float32
    )
    return lax.psum_scatter(
        partial_value.astype(jnp.bfloat16), "section", scatter_dimension=1, tiled=True
    ).astype(jnp.float32)


def back_of(masked_share, jac_block):
    masked_bf = lax.all_gather(masked_share, "section", axis=1, tiled=True)
    partial_value = jnp.dot(masked_bf, jac_block, preferred_element_type=jnp.float32)
    owned = lax.psum_scatter(
        partial_value.astype(jnp.bfloat16), "wave", scatter_dimension=1, tiled=True
    ).astype(jnp.float32)
    return lax.all_gather(owned, "wave", axis=1, tiled=True)


def reduce_scalars(values):
    return lax.psum(values, "section")


def general_shards(nominal_field, sensitivity, aberrations, jacobian, tile_mask, regul, initial_commands):
    components = jacobian.shape[1]
    pixels = jacobian.shape[2]
    block_width = jacobian.shape[3]
    row_count = components * pixels
    share_rows = row_count // lax.axis_size("section")
    row_start = lax.axis_index("section") * share_rows
    jac_block = jacobian.reshape(row_count, block_width)
    tile_count = tile_mask.shape[1]
    weight_full = jnp.broadcast_to(
        tile_mask[0].astype(jnp.float32)[None, :, None],
        (components, tile_count, pixels // tile_count),
    ).reshape(1, row_count)
    weight = lax.dynamic_slice_in_dim(weight_full, row_start, share_rows, 1)
    mode_count = sensitivity.shape[1]
    sens_share = lax.dynamic_slice_in_dim(
        sensitivity.reshape(mode_count, row_count), row_start, share_rows, 1
    )
    nominal_share = lax.dynamic_slice_in_dim(
        nominal_field.reshape(1, row_count), row_start, share_rows, 1
    )
    field_now = nominal_share + jnp.dot(aberrations, sens_share, preferred_element_type=jnp.float32)
    commands = initial_commands
    field_now = field_now + to_section_image(commands.astype(jnp.bfloat16), jac_block)
    for iteration in range(ITERS):
        residual = -back_of((weight * field_now).astype(jnp.bfloat16), jac_block)
        direction = residual
        change = jnp.zeros_like(residual)
        field_step = jnp.zeros_like(field_now)
        norm_now = reduce_scalars(jnp.sum(residual * residual, axis=1))
        for inner_step in range(CG):
            image_now = to_section_image(direction.astype(jnp.bfloat16), jac_block)
            applied = (
                back_of((weight * image_now).astype(jnp.bfloat16), jac_block)
                + regul[None, :] * direction
            )
            curvature = reduce_scalars(jnp.sum(direction * applied, axis=1))
            step_len = norm_now / (curvature + epsilon)
            residual = residual - step_len[:, None] * applied
            norm_next = reduce_scalars(jnp.sum(residual * residual, axis=1))
            change = change + step_len[:, None] * direction
            field_step = field_step + step_len[:, None] * image_now
            direction = residual + (norm_next / (norm_now + epsilon))[:, None] * direction
            norm_now = norm_next
        commands = commands + change
        field_now = field_now + field_step
    whole_field = lax.all_gather(
        field_now.astype(jnp.bfloat16), "section", axis=1, tiled=True
    ).astype(field_now.dtype)
    return (commands, whole_field.reshape(whole_field.shape[0], 1, components, pixels))


def control_kernel(
    n,
    jac_hbm,
    base_ref,
    start_ref,
    regul_ref,
    tile_ref,
    nominal_ref,
    cmd_ref,
    out_ref,
    jac,
    jact,
    probe,
    wpart,
    wrecv,
    ipart,
    crecv,
    xsend,
    xrecv,
    masked,
    img,
    field,
    qown,
    direction,
    change,
    residual,
    acc,
    gamma,
    rho,
    kappas,
    other,
    lost,
    owed,
    opart,
    orecv,
    weight_ref,
    jac_sem,
    cs_s,
    cs_r,
    xx_s,
    xx_r,
    cg_s,
    cg_r,
    ws_s,
    ws_r,
    ag_s,
    ag_r,
    fin_s,
    fin_r,
    out_s,
    out_r,
    ow_s,
    ow_r,
):
    f32, bf16 = jnp.float32, jnp.bfloat16
    half, acts = jac.shape[1:]
    mo = probe.shape[2]
    m = OWNERS * mo
    ac = acts // CHUNKS
    last = ITERS * CG
    sec, wav = lax.axis_index("section"), lax.axis_index("wave")
    core = lax.rem(sec, 2)
    sibling = {"section": sec + 1 - 2 * core}
    across = {"section": lax.rem(sec + 2, n)}
    first_owner = n // 2 - 1
    owners = [first_owner + o for o in range(OWNERS)]
    is_owner = jnp.logical_and(wav >= owners[0], wav <= owners[-1])
    far = jnp.where(wav <= first_owner, 1, 0)
    mine = jnp.clip(wav - first_owner, 0, OWNERS - 1)
    peers = range(n - 1)
    wav_peer = [{"wave": lax.rem(wav + k + 1, n)} for k in peers]

    block = half // BLOCKS

    def load(side, i):
        at = pl.multiple_of((core if side == 0 else 1 - core) * half + i * block, block)
        return pltpu.make_async_copy(
            jac_hbm.at[pl.ds(at, block)], jac.at[side, pl.ds(i * block, block)], jac_sem.at[side, i]
        )

    for side in (1, 0):
        for i in range(BLOCKS):
            load(side, i).start()
    barrier = pltpu.get_barrier_semaphore()
    slanted = [{"wave": lax.rem(wav + k + 1, n), **sibling} for k in peers]
    final_peer = slanted + wav_peer + [sibling]
    greeted = final_peer + [across]
    for p in greeted:
        pl.semaphore_signal(barrier, inc=1, device_id=p, device_id_type=pl.DeviceIdType.MESH)
    pl.semaphore_wait(barrier, len(greeted))

    def remote(src, dst, ss, rs, device):
        return pltpu.make_async_remote_copy(
            src_ref=src, dst_ref=dst, send_sem=ss, recv_sem=rs,
            device_id=device, device_id_type=pl.DeviceIdType.MESH,
        )

    def part_cols(c):
        return pl.ds(0, SIDE + ac) if c == 0 else pl.ds(SIDE + c * ac, ac)

    def core_sum(s):
        return remote(ipart.at[s], crecv.at[s], cs_s.at[s], cs_r.at[s], sibling)

    def x_sum(s, slot):
        return remote(xsend.at[s], xrecv.at[slot, s], xx_s.at[slot, s], xx_r.at[slot, s], across)

    def core_share(s):
        return remote(masked.at[s, 0], masked.at[s, 1], cg_s.at[s], cg_r.at[s], sibling)

    def to_owner(s, c, o):
        owner = first_owner + o
        k = lax.rem(wav - owner + n - 1 + n, n)
        return remote(
            wpart.at[s, o, :, part_cols(c)],
            wrecv.at[s, k, :, part_cols(c)],
            ws_s.at[s, c, o],
            ws_r.at[s, c, k],
            {"wave": owner},
        )

    def owed_copy(s, o):
        owner = first_owner + o
        k = lax.rem(wav - owner + n - 1 + n, n)
        return remote(
            opart.at[s, o], orecv.at[s, k], ow_s.at[s, o], ow_r.at[s, k], {"wave": owner}
        )

    def owed_at(s, k):
        return remote(opart.at[s, 0], orecv.at[s, k], ow_s.at[s, 0], ow_r.at[s, k], wav_peer[0])

    def at_owner(s, c, k):
        return remote(
            wpart.at[s, 0, :, part_cols(c)],
            wrecv.at[s, k, :, part_cols(c)],
            ws_s.at[s, c, 0],
            ws_r.at[s, c, k],
            wav_peer[0],
        )

    def from_owner(s, c, o, k):
        return remote(
            probe.at[s, o, :, part_cols(c)],
            probe.at[s, o, :, part_cols(c)],
            ag_s.at[s, c, k],
            ag_r.at[s, c, o],
            wav_peer[k],
        )

    def kappa_copy(s, k):
        return remote(
            kappas.at[wav, core, s],
            kappas.at[wav, core, s],
            fin_s.at[s, k],
            fin_r.at[s, k],
            final_peer[k],
        )

    def out_copy(s, at):
        return remote(
            (field, img)[at].at[s], other.at[s, at], out_s.at[s, at], out_r.at[s, at], sibling
        )

    def row_sum(values):
        return jnp.sum(values, axis=1, keepdims=True)

    def pack(values):
        lane = lax.broadcasted_iota(jnp.int32, (values[0].shape[0], SIDE), 1)
        packed = jnp.zeros(lane.shape, f32)
        for at, value in enumerate(values):
            rest = value
            for piece in range(3):
                top = rest.astype(bf16).astype(f32)
                rest = rest - top
                packed = jnp.where(lane == 3 * at + piece, top, packed)
        return packed.astype(bf16)

    def beside(block, more):
        return block.astype(f32) + pltpu.roll(more.astype(f32), 16, 1)

    def pick(lanes, at):
        lane = lax.rem(lax.broadcasted_iota(jnp.int32, lanes.shape, 1), 16)
        return row_sum(jnp.where(jnp.logical_and(lane >= 3 * at, lane < 3 * at + 3), lanes, 0.0))

    def spread(column):
        return jnp.broadcast_to(column, (column.shape[0], LANES))

    def dot(lhs, rhs):
        padded = jnp.concatenate([lhs, jnp.zeros((PAD - m, lhs.shape[1]), bf16)], axis=0)
        return jnp.dot(padded, rhs, preferred_element_type=f32)[:m]

    def make_image(s, k):
        def arrive(c):
            @pl.when(k > 0)
            def _():
                for o in range(OWNERS):
                    @pl.when(wav != owners[o])
                    def _():
                        from_owner(s, c, o, 0).wait_recv()

        def scalars(c, lhs):
            cols = slice(c * ac, (c + 1) * ac)
            wide = lhs.astype(f32)
            scaled = regul_ref[:, cols] * wide
            along = direction[s, :, :, cols].reshape(m, ac)
            return [row_sum(wide * wide), row_sum(scaled * wide), row_sum(scaled * along)]

        sums = None
        for c in range(CHUNKS):
            arrive(c)
            lhs = probe[s, :, :, SIDE + c * ac:SIDE + (c + 1) * ac].reshape(m, ac)
            more = scalars(c, lhs)
            sums = more if sums is None else [x + y for x, y in zip(sums, more)]
            for side in (1, 0):
                part = dot(lhs, jact[side, c * ac:(c + 1) * ac, :])
                cols = slice(side * half, (side + 1) * half)
                if c:
                    part = acc[:, cols] + part
                if c < CHUNKS - 1:
                    acc[:, cols] = part
                elif side == 1:
                    ipart[s, :, 0:SIDE] = pack(sums)
                    ipart[s, :, SIDE:] = part.astype(bf16)
                    core_sum(s).start()
                else:
                    qown[s] = part
        step = row_sum(probe[s, :, :, 0:SIDE].reshape(m, SIDE).astype(f32))
        field[s] = field[s] + step * img[s]
        step = step.reshape(OWNERS, mo, 1)
        change[s] = change[s] + step * direction[s]
        owed[s] = owed[s] + step * lost[s]

    def settle(s):
        for p in peers:
            owed_at(s, p).wait_recv()
        total = opart[s, mine].astype(f32)
        for p in peers:
            total = total + orecv[s, p].astype(f32)
        residual[s] = residual[s] - total

    def join_cores(s, k):
        core_sum(s).wait()
        xsend[s, :, 0:SIDE] = beside(ipart[s, :, 0:SIDE], crecv[s, :, 0:SIDE]).astype(bf16)
        xsend[s, :, SIDE:] = (qown[s] + crecv[s, :, SIDE:].astype(f32)).astype(bf16)
        x_sum(s, lax.rem(k, 2)).start()

        @pl.when(k == CG)
        def _():
            opart[s] = owed[s].astype(bf16)
            owed_copy(s, far).start()

            @pl.when(jnp.logical_not(is_owner))
            def _():
                owed_copy(s, 1 - far).start()

    def take_image(s, k):
        slot = lax.rem(k, 2)
        x_sum(s, slot).wait()
        lanes = xsend[s, :, 0:SIDE].astype(f32) + xrecv[slot, s, :, 0:SIDE].astype(f32)
        norm, aa, bb = [pick(lanes, at) for at in range(3)]
        norm_before = gamma[s].reshape(m, LANES)[:, 0:1]
        rho_before = rho[s].reshape(m, LANES)[:, 0:1]
        ratio = norm / (norm_before + epsilon)
        ratio = jnp.where(lax.rem(k, CG) == 1, 0.0, ratio)
        ratio = jnp.where(k == 0, 1.0, ratio)
        rho_now = jnp.maximum(aa + 2.0 * ratio * bb + ratio * ratio * rho_before, 0.0)
        gamma[s] = spread(norm).reshape(OWNERS, mo, LANES)
        rho[s] = spread(rho_now).reshape(OWNERS, mo, LANES)
        now = xsend[s, :, SIDE:].astype(f32) + xrecv[slot, s, :, SIDE:].astype(f32) + ratio * img[s]
        img[s] = now
        kept = (weight_ref[...] * now).astype(bf16)
        masked[s, 0] = kept

        @pl.when(k < last)
        def _():
            core_share(s).start()

        fresh = jnp.where(k == 0, 0.0, 1.0)
        direction[s] = (
            fresh * probe[s, :, :, SIDE:].astype(f32) + ratio.reshape(OWNERS, mo, 1) * direction[s]
        )

        @pl.when(k > 0)
        def _():
            for c in range(CHUNKS):
                to_owner(s, c, far).wait_send()

                @pl.when(jnp.logical_not(is_owner))
                def _():
                    to_owner(s, c, 1 - far).wait_send()

            @pl.when(is_owner)
            def _():
                for c in range(CHUNKS):
                    for p in peers:
                        from_owner(s, c, mine, p).wait_send()

            @pl.when(k == CG + 1)
            def _():
                owed_copy(s, far).wait_send()

                @pl.when(jnp.logical_not(is_owner))
                def _():
                    owed_copy(s, 1 - far).wait_send()

    def square(s, side):
        wide = masked[s, side].astype(f32)
        return row_sum(wide * wide)

    def make_back(s):
        lhs = masked[s, 0]
        for c in range(CHUNKS):
            cols = slice(c * ac, (c + 1) * ac)
            acc[:, cols] = dot(lhs, jac[0, :, cols])
        kappa = square(s, 0)
        core_share(s).wait()
        kappa = pack([kappa + square(s, 1)])
        wpart[s, :, :, 0:SIDE] = kappa.reshape(OWNERS, mo, SIDE)
        lhs = masked[s, 1]
        for c in range(CHUNKS):
            cols = slice(c * ac, (c + 1) * ac)
            part = acc[:, cols] + dot(lhs, jac[1, :, cols])
            sent = part.astype(bf16)
            wpart[s, :, :, SIDE + c * ac:SIDE + (c + 1) * ac] = sent.reshape(OWNERS, mo, ac)
            to_owner(s, c, far).start()

            @pl.when(jnp.logical_not(is_owner))
            def _():
                to_owner(s, c, 1 - far).start()

            lost[s, :, :, cols] = (part - sent.astype(f32)).reshape(OWNERS, mo, ac)

    def update(s, k):
        @pl.when(is_owner)
        def _():
            again = jnp.where(k == CG, 1.0, 0.0)

            @pl.when(k == CG)
            def _():
                settle(s)

            for c in range(CHUNKS):
                for p in peers:
                    at_owner(s, c, p).wait_recv()
                if c == 0:
                    kappa = wpart[s, mine, :, 0:SIDE].astype(f32)
                    for p in peers:
                        kappa = kappa + wrecv[s, p, :, 0:SIDE].astype(f32)
                    kappa = row_sum(kappa)
                    norm, rho_now = gamma[s, mine][:, 0:1], rho[s, mine][:, 0:1]
                    step = norm / (kappa + rho_now + epsilon)
                    step = jnp.where(k == 0, 1.0, step)
                    probe[s, mine, :, 0:SIDE] = pack([step])
                cols = slice(c * ac, (c + 1) * ac)
                wide = slice(SIDE + c * ac, SIDE + (c + 1) * ac)
                total = wpart[s, mine, :, wide].astype(f32)
                for p in peers:
                    total = total + wrecv[s, p, :, wide].astype(f32)
                along = direction[s, mine, :, cols]
                weight = regul_ref[:, cols]
                after = residual[s, :, cols] - step * (total + weight * along)
                after = after + again * (weight * (change[s, mine, :, cols] + step * along))
                residual[s, :, cols] = after
                probe[s, mine, :, wide] = after.astype(bf16)
                for p in (1, 0, 2):
                    from_owner(s, c, mine, p).start()

    def send_kappa(s):
        for at in range(2):
            out_copy(s, at).start()
        kappas[wav, core, s] = pack([square(s, 0)])
        for p in range(len(final_peer)):
            kappa_copy(s, p).start()

    def finish(s):
        for p in range(len(final_peer)):
            kappa_copy(s, p).wait()
        kappa = jnp.zeros((m, SIDE), f32)
        for w in range(n):
            for c in range(2):
                kappa = kappa + kappas[w, c, s].astype(f32)
        step = gamma[s].reshape(m, LANES)[:, 0:1]
        step = step / (row_sum(kappa) + rho[s].reshape(m, LANES)[:, 0:1] + epsilon)
        rows = pl.ds(s * m, m)
        moved = change[s] + step.reshape(OWNERS, mo, 1) * direction[s]
        cmd_ref[rows, :] = start_ref[rows, :] + moved.reshape(m, acts)
        for at in range(2):
            out_copy(s, at).wait()
        here = field[s] + step * img[s]
        there = other[s, 0] + step * other[s, 1]
        out_ref[rows, 0, :] = jnp.where(core == 0, here, there)
        out_ref[rows, 1, :] = jnp.where(core == 0, there, here)

    for s in range(STREAMS):
        probe[s, :, :, 0:SIDE] = jnp.zeros((OWNERS, mo, SIDE), bf16)
        probe[s, :, :, SIDE:] = start_ref[s * m:(s + 1) * m, :].astype(bf16).reshape(OWNERS, mo, acts)
        nominal = jnp.where(core == 0, nominal_ref[0:1, :], nominal_ref[1:2, :])
        img[s] = nominal + base_ref[s * m:(s + 1) * m, :]
    tiles = tile_ref.shape[1]
    wide = half // tiles
    for tile in range(tiles):
        weight_ref[:, tile * wide:(tile + 1) * wide] = jnp.full(
            (1, wide), tile_ref[0, tile].astype(f32), f32
        )
    for ref in (field, direction, change, residual, gamma, rho, lost, owed):
        ref[...] = jnp.zeros_like(ref)
    lhs = probe[0, :, :, SIDE:].reshape(m, acts)
    for side in (1, 0):
        for i in range(BLOCKS):
            load(side, i).wait()
        part = lax.dot_general(
            lhs, jac[side], (((1,), (1,)), ((), ())), preferred_element_type=f32
        )
        if side == 1:
            ipart[0, :, 0:SIDE] = jnp.zeros((m, SIDE), bf16)
            ipart[0, :, SIDE:] = part.astype(bf16)
            core_sum(0).start()
        else:
            qown[0] = part
    join_cores(0, 0)

    def turn(i, carry):
        for side in range(2):
            at = pl.multiple_of(i * block, block)
            jact[side, :, pl.ds(at, block)] = jac[side, pl.ds(at, block), :].T
        return carry

    lax.fori_loop(0, BLOCKS, turn, 0)

    def turn_half(t, carry):
        here, there = lax.rem(t + 1, 2), lax.rem(t, 2)
        k_here = (t + 1) // 2 - 1
        k_there = t // 2

        @pl.when(t >= 2)
        def _():
            join_cores(here, k_here)

        @pl.when(jnp.logical_and(t >= 2, t <= 2 * last + 1))
        def _():
            update(there, k_there - 1)

        @pl.when(t == 2 * last + 2)
        def _():
            finish(0)

        take_image(here, k_here)

        @pl.when(t <= 2 * last)
        def _():
            make_back(here)

        @pl.when(t > 2 * last)
        def _():
            send_kappa(here)

        @pl.when(t <= 2 * last + 1)
        def _():
            make_image(there, k_there)

        return carry

    lax.fori_loop(1, 2 * last + 3, turn_half, 0)
    finish(1)


def kernel_shards(nominal_field, sensitivity, aberrations, jacobian, tile_mask, regul, initial_commands):
    f32, bf16 = jnp.float32, jnp.bfloat16
    components, pixels, acts = jacobian.shape[1:]
    rows = components * pixels
    half = pixels
    reals = initial_commands.shape[0]
    n = lax.axis_size("section")
    m = reals // STREAMS
    mo = m // OWNERS
    core = lax.rem(lax.axis_index("section"), 2)
    mine = (jnp.arange(components) == core).astype(bf16)
    base = lax.dot_general(
        aberrations[:, :, None] * mine,
        sensitivity[0],
        (((1, 2), (0, 1)), ((), ())),
        preferred_element_type=f32,
    )
    vmem = pl.BlockSpec(memory_space=pltpu.VMEM)
    dma = pltpu.SemaphoreType.DMA
    commands, field = pl.pallas_call(
        functools.partial(control_kernel, n),
        out_shape=(
            jax.ShapeDtypeStruct((reals, acts), f32),
            jax.ShapeDtypeStruct((reals, components, pixels), f32),
        ),
        in_specs=[
            pl.BlockSpec(memory_space=pl.ANY),
            vmem,
            vmem,
            vmem,
            pl.BlockSpec(memory_space=pltpu.SMEM),
            vmem,
        ],
        out_specs=(vmem, vmem),
        scratch_shapes=[
            pltpu.VMEM((2, half, acts), bf16),
            pltpu.VMEM((2, acts, half), bf16),
            pltpu.VMEM((STREAMS, OWNERS, mo, SIDE + acts), bf16),
            pltpu.VMEM((STREAMS, OWNERS, mo, SIDE + acts), bf16),
            pltpu.VMEM((STREAMS, n - 1, mo, SIDE + acts), bf16),
            pltpu.VMEM((STREAMS, m, SIDE + half), bf16),
            pltpu.VMEM((STREAMS, m, SIDE + half), bf16),
            pltpu.VMEM((STREAMS, m, SIDE + half), bf16),
            pltpu.VMEM((2, STREAMS, m, SIDE + half), bf16),
            pltpu.VMEM((STREAMS, 2, m, half), bf16),
            pltpu.VMEM((STREAMS, m, half), f32),
            pltpu.VMEM((STREAMS, m, half), f32),
            pltpu.VMEM((STREAMS, m, half), f32),
            pltpu.VMEM((STREAMS, OWNERS, mo, acts), f32),
            pltpu.VMEM((STREAMS, OWNERS, mo, acts), f32),
            pltpu.VMEM((STREAMS, mo, acts), f32),
            pltpu.VMEM((m, max(2 * half, acts)), f32),
            pltpu.VMEM((STREAMS, OWNERS, mo, LANES), f32),
            pltpu.VMEM((STREAMS, OWNERS, mo, LANES), f32),
            pltpu.VMEM((n, 2, STREAMS, m, SIDE), bf16),
            pltpu.VMEM((STREAMS, 2, m, half), f32),
            pltpu.VMEM((STREAMS, OWNERS, mo, acts), f32),
            pltpu.VMEM((STREAMS, OWNERS, mo, acts), f32),
            pltpu.VMEM((STREAMS, OWNERS, mo, acts), bf16),
            pltpu.VMEM((STREAMS, n - 1, mo, acts), bf16),
            pltpu.VMEM((1, half), f32),
            dma((2, BLOCKS)),
            dma((STREAMS,)),
            dma((STREAMS,)),
            dma((2, STREAMS)),
            dma((2, STREAMS)),
            dma((STREAMS,)),
            dma((STREAMS,)),
            dma((STREAMS, CHUNKS, OWNERS)),
            dma((STREAMS, CHUNKS, n - 1)),
            dma((STREAMS, CHUNKS, n - 1)),
            dma((STREAMS, CHUNKS, OWNERS)),
            dma((STREAMS, 2 * n - 1)),
            dma((STREAMS, 2 * n - 1)),
            dma((STREAMS, 2)),
            dma((STREAMS, 2)),
            dma((STREAMS, OWNERS)),
            dma((STREAMS, n - 1)),
        ],
        compiler_params=pltpu.CompilerParams(
            collective_id=0, has_side_effects=True, vmem_limit_bytes=48 * 1024 * 1024
        ),
        name="control_loop",
    )(
        jacobian.reshape(rows, acts),
        base,
        initial_commands,
        regul[None, :],
        tile_mask,
        nominal_field[0],
    )
    return commands, field.reshape(reals, 1, components, pixels)


def solution(mesh):
    placed = (
        P("wave", None, None),
        P("wave", None, None, None),
        P("groups", None),
        P("wave", None, None, "section"),
        P("wave", None),
        P("section"),
        P("groups", "section"),
    )

    def choose(*args):
        n, waves = mesh.shape["section"], mesh.shape["wave"]
        reals = args[6].shape[0]
        acts = args[3].shape[3]
        pixels = args[3].shape[2]
        fits = (
            n == 4
            and waves == 4
            and args[3].shape[1] == 2
            and reals % (16 * STREAMS * OWNERS) == 0
            and acts % (LANES * CHUNKS) == 0
            and pixels % (LANES * args[4].shape[1]) == 0
            and 2 * pixels * acts <= 2048 * 2048
            and reals <= 64
        )
        return (kernel_shards if fits else general_shards)(*args)

    return jax.shard_map(
        choose,
        mesh=mesh,
        in_specs=placed,
        out_specs=(P("groups", "section"), P("groups", "wave", None, None)),
        check_vma=False,
    )
```

```python
import functools

import jax
import jax.numpy as jnp
from jax import lax
from jax.experimental import pallas as pl
from jax.experimental.pallas import tpu as pltpu
from jax.sharding import PartitionSpec as P

ITERS = 2
CG = 5
LANES = 128
CHUNKS = 2
STREAMS = 2
OWNERS = 2
SIDE = 128
BLOCKS = 4
PAD = 128

epsilon = 1e-06


def to_section_image(command_bf, jac_block):
    partial_value = lax.dot_general(
        command_bf, jac_block, (((1,), (1,)), ((), ())), preferred_element_type=jnp.float32
    )
    return lax.psum_scatter(
        partial_value.astype(jnp.bfloat16), "section", scatter_dimension=1, tiled=True
    ).astype(jnp.float32)


def back_of(masked_share, jac_block):
    masked_bf = lax.all_gather(masked_share, "section", axis=1, tiled=True)
    partial_value = jnp.dot(masked_bf, jac_block, preferred_element_type=jnp.float32)
    owned = lax.psum_scatter(
        partial_value.astype(jnp.bfloat16), "wave", scatter_dimension=1, tiled=True
    ).astype(jnp.float32)
    return lax.all_gather(owned, "wave", axis=1, tiled=True)


def reduce_scalars(values):
    return lax.psum(values, "section")


def general_shards(nominal_field, sensitivity, aberrations, jacobian, tile_mask, regul, initial_commands):
    components = jacobian.shape[1]
    pixels = jacobian.shape[2]
    block_width = jacobian.shape[3]
    row_count = components * pixels
    share_rows = row_count // lax.axis_size("section")
    row_start = lax.axis_index("section") * share_rows
    jac_block = jacobian.reshape(row_count, block_width)
    tile_count = tile_mask.shape[1]
    weight_full = jnp.broadcast_to(
        tile_mask[0].astype(jnp.float32)[None, :, None],
        (components, tile_count, pixels // tile_count),
    ).reshape(1, row_count)
    weight = lax.dynamic_slice_in_dim(weight_full, row_start, share_rows, 1)
    mode_count = sensitivity.shape[1]
    sens_share = lax.dynamic_slice_in_dim(
        sensitivity.reshape(mode_count, row_count), row_start, share_rows, 1
    )
    nominal_share = lax.dynamic_slice_in_dim(
        nominal_field.reshape(1, row_count), row_start, share_rows, 1
    )
    field_now = nominal_share + jnp.dot(aberrations, sens_share, preferred_element_type=jnp.float32)
    commands = initial_commands
    field_now = field_now + to_section_image(commands.astype(jnp.bfloat16), jac_block)
    for iteration in range(ITERS):
        residual = -back_of((weight * field_now).astype(jnp.bfloat16), jac_block)
        direction = residual
        change = jnp.zeros_like(residual)
        field_step = jnp.zeros_like(field_now)
        norm_now = reduce_scalars(jnp.sum(residual * residual, axis=1))
        for inner_step in range(CG):
            image_now = to_section_image(direction.astype(jnp.bfloat16), jac_block)
            applied = (
                back_of((weight * image_now).astype(jnp.bfloat16), jac_block)
                + regul[None, :] * direction
            )
            curvature = reduce_scalars(jnp.sum(direction * applied, axis=1))
            step_len = norm_now / (curvature + epsilon)
            residual = residual - step_len[:, None] * applied
            norm_next = reduce_scalars(jnp.sum(residual * residual, axis=1))
            change = change + step_len[:, None] * direction
            field_step = field_step + step_len[:, None] * image_now
            direction = residual + (norm_next / (norm_now + epsilon))[:, None] * direction
            norm_now = norm_next
        commands = commands + change
        field_now = field_now + field_step
    whole_field = lax.all_gather(
        field_now.astype(jnp.bfloat16), "section", axis=1, tiled=True
    ).astype(field_now.dtype)
    return (commands, whole_field.reshape(whole_field.shape[0], 1, components, pixels))


def control_kernel(
    n,
    jac_hbm,
    base_ref,
    start_ref,
    regul_ref,
    tile_ref,
    nominal_ref,
    cmd_ref,
    out_ref,
    jac,
    jact,
    probe,
    wpart,
    wrecv,
    ipart,
    crecv,
    xsend,
    xrecv,
    masked,
    img,
    field,
    qown,
    direction,
    change,
    residual,
    acc,
    gamma,
    rho,
    kappas,
    other,
    lost,
    owed,
    opart,
    orecv,
    weight_ref,
    scal,
    jac_sem,
    cs_s,
    cs_r,
    xx_s,
    xx_r,
    cg_s,
    cg_r,
    ws_s,
    ws_r,
    ag_s,
    ag_r,
    fin_s,
    fin_r,
    out_s,
    out_r,
    ow_s,
    ow_r,
    sc_s,
    sc_r,
):
    f32, bf16 = jnp.float32, jnp.bfloat16
    half, acts = jac.shape[1:]
    mo = probe.shape[2]
    m = OWNERS * mo
    ac = acts // CHUNKS
    last = ITERS * CG
    sec, wav = lax.axis_index("section"), lax.axis_index("wave")
    core = lax.rem(sec, 2)
    sibling = {"section": sec + 1 - 2 * core}
    across = {"section": lax.rem(sec + 2, n)}
    first_owner = n // 2 - 1
    owners = [first_owner + o for o in range(OWNERS)]
    is_owner = jnp.logical_and(wav >= owners[0], wav <= owners[-1])
    far = jnp.where(wav <= first_owner, 1, 0)
    mine = jnp.clip(wav - first_owner, 0, OWNERS - 1)
    peers = range(n - 1)
    wav_peer = [{"wave": lax.rem(wav + k + 1, n)} for k in peers]

    block = half // BLOCKS

    def load(side, i):
        at = pl.multiple_of((core if side == 0 else 1 - core) * half + i * block, block)
        return pltpu.make_async_copy(
            jac_hbm.at[pl.ds(at, block)], jac.at[side, pl.ds(i * block, block)], jac_sem.at[side, i]
        )

    for side in (1, 0):
        for i in range(BLOCKS):
            load(side, i).start()
    barrier = pltpu.get_barrier_semaphore()
    slanted = [{"wave": lax.rem(wav + k + 1, n), **sibling} for k in peers]
    final_peer = slanted + wav_peer + [sibling]
    opposite = {"section": lax.rem(sec + 3 - 2 * core, n)}
    greeted = final_peer + [across, opposite]
    for p in greeted:
        pl.semaphore_signal(barrier, inc=1, device_id=p, device_id_type=pl.DeviceIdType.MESH)
    pl.semaphore_wait(barrier, len(greeted))

    def remote(src, dst, ss, rs, device):
        return pltpu.make_async_remote_copy(
            src_ref=src, dst_ref=dst, send_sem=ss, recv_sem=rs,
            device_id=device, device_id_type=pl.DeviceIdType.MESH,
        )

    def part_cols(c):
        return pl.ds(0, SIDE + ac) if c == 0 else pl.ds(SIDE + c * ac, ac)

    def core_sum(s):
        return remote(ipart.at[s], crecv.at[s], cs_s.at[s], cs_r.at[s], sibling)

    def x_sum(s, slot):
        return remote(xsend.at[s], xrecv.at[slot, s], xx_s.at[slot, s], xx_r.at[slot, s], across)

    def scal_copy(s, slot, k):
        return remote(
            scal.at[slot, sec, s],
            scal.at[slot, sec, s],
            sc_s.at[slot, s, k],
            sc_r.at[slot, s, k],
            {"section": lax.rem(sec + k + 1, n)},
        )

    def core_share(s):
        return remote(masked.at[s, 0], masked.at[s, 1], cg_s.at[s], cg_r.at[s], sibling)

    def to_owner(s, c, o):
        owner = first_owner + o
        k = lax.rem(wav - owner + n - 1 + n, n)
        return remote(
            wpart.at[s, o, :, part_cols(c)],
            wrecv.at[s, k, :, part_cols(c)],
            ws_s.at[s, c, o],
            ws_r.at[s, c, k],
            {"wave": owner},
        )

    def owed_copy(s, o):
        owner = first_owner + o
        k = lax.rem(wav - owner + n - 1 + n, n)
        return remote(
            opart.at[s, o], orecv.at[s, k], ow_s.at[s, o], ow_r.at[s, k], {"wave": owner}
        )

    def owed_at(s, k):
        return remote(opart.at[s, 0], orecv.at[s, k], ow_s.at[s, 0], ow_r.at[s, k], wav_peer[0])

    def at_owner(s, c, k):
        return remote(
            wpart.at[s, 0, :, part_cols(c)],
            wrecv.at[s, k, :, part_cols(c)],
            ws_s.at[s, c, 0],
            ws_r.at[s, c, k],
            wav_peer[0],
        )

    def from_owner(s, c, o, k):
        return remote(
            probe.at[s, o, :, part_cols(c)],
            probe.at[s, o, :, part_cols(c)],
            ag_s.at[s, c, k],
            ag_r.at[s, c, o],
            wav_peer[k],
        )

    def kappa_copy(s, k):
        return remote(
            kappas.at[wav, core, s],
            kappas.at[wav, core, s],
            fin_s.at[s, k],
            fin_r.at[s, k],
            final_peer[k],
        )

    def out_copy(s, at):
        return remote(
            (field, img)[at].at[s], other.at[s, at], out_s.at[s, at], out_r.at[s, at], sibling
        )

    def row_sum(values):
        return jnp.sum(values, axis=1, keepdims=True)

    def pack(values):
        lane = lax.broadcasted_iota(jnp.int32, (values[0].shape[0], SIDE), 1)
        packed = jnp.zeros(lane.shape, f32)
        for at, value in enumerate(values):
            rest = value
            for piece in range(3):
                top = rest.astype(bf16).astype(f32)
                rest = rest - top
                packed = jnp.where(lane == 3 * at + piece, top, packed)
        return packed.astype(bf16)

    def spread(column):
        return jnp.broadcast_to(column, (column.shape[0], LANES))

    def dot(lhs, rhs):
        padded = jnp.concatenate([lhs, jnp.zeros((PAD - m, lhs.shape[1]), bf16)], axis=0)
        return jnp.dot(padded, rhs, preferred_element_type=f32)[:m]

    def send_scalars(s, k, sums):
        lane = lax.broadcasted_iota(jnp.int32, (m, LANES), 1)
        packed = jnp.zeros((m, LANES), f32)
        for at, value in enumerate(sums):
            packed = jnp.where(lane == at, value, packed)
        slot = lax.rem(k, 2)
        scal[slot, sec, s] = packed
        for p in peers:
            scal_copy(s, slot, p).start()

    def make_image(s, k):
        def arrive(c):
            @pl.when(k > 0)
            def _():
                for o in range(OWNERS):
                    @pl.when(wav != owners[o])
                    def _():
                        from_owner(s, c, o, 0).wait_recv()

        def scalars(c, lhs):
            cols = slice(c * ac, (c + 1) * ac)
            wide = lhs.astype(f32)
            scaled = regul_ref[:, cols] * wide
            along = direction[s, :, :, cols].reshape(m, ac)
            return [row_sum(wide * wide), row_sum(scaled * wide), row_sum(scaled * along)]

        sums = None
        for c in range(CHUNKS):
            arrive(c)
            lhs = probe[s, :, :, SIDE + c * ac:SIDE + (c + 1) * ac].reshape(m, ac)
            for side in (1, 0):
                part = dot(lhs, jact[side, c * ac:(c + 1) * ac, :])
                cols = slice(side * half, (side + 1) * half)
                if c:
                    part = acc[:, cols] + part
                if c < CHUNKS - 1:
                    acc[:, cols] = part
                elif side == 1:
                    ipart[s] = part.astype(bf16)
                    core_sum(s).start()
                else:
                    qown[s] = part
                if side == 1:
                    more = scalars(c, lhs)
                    sums = more if sums is None else [x + y for x, y in zip(sums, more)]
                    if c == CHUNKS - 1:
                        send_scalars(s, k, sums)
        step = row_sum(probe[s, :, :, 0:SIDE].reshape(m, SIDE).astype(f32))
        field[s] = field[s] + step * img[s]
        step = step.reshape(OWNERS, mo, 1)
        change[s] = change[s] + step * direction[s]
        owed[s] = owed[s] + step * lost[s]

    def settle(s):
        for p in peers:
            owed_at(s, p).wait_recv()
        total = opart[s, mine].astype(f32)
        for p in peers:
            total = total + orecv[s, p].astype(f32)
        residual[s] = residual[s] - total

    def join_cores(s, k):
        core_sum(s).wait()
        xsend[s] = (qown[s] + crecv[s].astype(f32)).astype(bf16)
        x_sum(s, lax.rem(k, 2)).start()

        @pl.when(k == CG)
        def _():
            opart[s] = owed[s].astype(bf16)
            owed_copy(s, far).start()

            @pl.when(jnp.logical_not(is_owner))
            def _():
                owed_copy(s, 1 - far).start()

    def take_image(s, k):
        slot = lax.rem(k, 2)
        for p in peers:
            scal_copy(s, slot, p).wait()
        lanes = scal[slot, 0, s]
        for at in range(1, n):
            lanes = lanes + scal[slot, at, s]
        norm, aa, bb = [lanes[:, at:at + 1] for at in range(3)]
        norm_before = gamma[s].reshape(m, LANES)[:, 0:1]
        rho_before = rho[s].reshape(m, LANES)[:, 0:1]
        ratio = norm / (norm_before + epsilon)
        ratio = jnp.where(lax.rem(k, CG) == 1, 0.0, ratio)
        ratio = jnp.where(k == 0, 1.0, ratio)
        rho_now = jnp.maximum(aa + 2.0 * ratio * bb + ratio * ratio * rho_before, 0.0)
        gamma[s] = spread(norm).reshape(OWNERS, mo, LANES)
        rho[s] = spread(rho_now).reshape(OWNERS, mo, LANES)
        fresh = jnp.where(k == 0, 0.0, 1.0)
        direction[s] = (
            fresh * probe[s, :, :, SIDE:].astype(f32) + ratio.reshape(OWNERS, mo, 1) * direction[s]
        )
        img[s] = ratio * img[s]
        @pl.when(k > 0)
        def _():
            for c in range(CHUNKS):
                to_owner(s, c, far).wait_send()

                @pl.when(jnp.logical_not(is_owner))
                def _():
                    to_owner(s, c, 1 - far).wait_send()

            @pl.when(is_owner)
            def _():
                for c in range(CHUNKS):
                    for p in peers:
                        from_owner(s, c, mine, p).wait_send()

            @pl.when(k == CG + 1)
            def _():
                owed_copy(s, far).wait_send()

                @pl.when(jnp.logical_not(is_owner))
                def _():
                    owed_copy(s, 1 - far).wait_send()

        x_sum(s, slot).wait()
        now = xsend[s].astype(f32) + xrecv[slot, s].astype(f32) + img[s]
        img[s] = now
        kept = (weight_ref[...] * now).astype(bf16)
        masked[s, 0] = kept

        @pl.when(k < last)
        def _():
            core_share(s).start()

    def square(s, side):
        wide = masked[s, side].astype(f32)
        return row_sum(wide * wide)

    def make_back(s):
        lhs = masked[s, 0]
        for c in range(CHUNKS):
            cols = slice(c * ac, (c + 1) * ac)
            acc[:, cols] = dot(lhs, jac[0, :, cols])
        kappa = square(s, 0)
        core_share(s).wait()
        kappa = pack([kappa + square(s, 1)])
        wpart[s, :, :, 0:SIDE] = kappa.reshape(OWNERS, mo, SIDE)
        lhs = masked[s, 1]
        for c in range(CHUNKS):
            cols = slice(c * ac, (c + 1) * ac)
            part = acc[:, cols] + dot(lhs, jac[1, :, cols])
            sent = part.astype(bf16)
            wpart[s, :, :, SIDE + c * ac:SIDE + (c + 1) * ac] = sent.reshape(OWNERS, mo, ac)
            to_owner(s, c, far).start()

            @pl.when(jnp.logical_not(is_owner))
            def _():
                to_owner(s, c, 1 - far).start()

            lost[s, :, :, cols] = (part - sent.astype(f32)).reshape(OWNERS, mo, ac)

    def update(s, k):
        @pl.when(is_owner)
        def _():
            again = jnp.where(k == CG, 1.0, 0.0)

            @pl.when(k == CG)
            def _():
                settle(s)

            for c in range(CHUNKS):
                for p in peers:
                    at_owner(s, c, p).wait_recv()
                if c == 0:
                    kappa = wpart[s, mine, :, 0:SIDE].astype(f32)
                    for p in peers:
                        kappa = kappa + wrecv[s, p, :, 0:SIDE].astype(f32)
                    kappa = row_sum(kappa)
                    norm, rho_now = gamma[s, mine][:, 0:1], rho[s, mine][:, 0:1]
                    step = norm / (kappa + rho_now + epsilon)
                    step = jnp.where(k == 0, 1.0, step)
                    probe[s, mine, :, 0:SIDE] = pack([step])
                cols = slice(c * ac, (c + 1) * ac)
                wide = slice(SIDE + c * ac, SIDE + (c + 1) * ac)
                total = wpart[s, mine, :, wide].astype(f32)
                for p in peers:
                    total = total + wrecv[s, p, :, wide].astype(f32)
                along = direction[s, mine, :, cols]
                weight = regul_ref[:, cols]
                after = residual[s, :, cols] - step * (total + weight * along)
                after = after + again * (weight * (change[s, mine, :, cols] + step * along))
                residual[s, :, cols] = after
                probe[s, mine, :, wide] = after.astype(bf16)
                for p in (1, 0, 2):
                    from_owner(s, c, mine, p).start()

    def send_kappa(s):
        for at in range(2):
            out_copy(s, at).start()
        kappas[wav, core, s] = pack([square(s, 0)])
        for p in range(len(final_peer)):
            kappa_copy(s, p).start()

    def finish(s):
        for p in range(len(final_peer)):
            kappa_copy(s, p).wait()
        kappa = jnp.zeros((m, SIDE), f32)
        for w in range(n):
            for c in range(2):
                kappa = kappa + kappas[w, c, s].astype(f32)
        step = gamma[s].reshape(m, LANES)[:, 0:1]
        step = step / (row_sum(kappa) + rho[s].reshape(m, LANES)[:, 0:1] + epsilon)
        rows = pl.ds(s * m, m)
        moved = change[s] + step.reshape(OWNERS, mo, 1) * direction[s]
        cmd_ref[rows, :] = start_ref[rows, :] + moved.reshape(m, acts)
        for at in range(2):
            out_copy(s, at).wait()
        here = field[s] + step * img[s]
        there = other[s, 0] + step * other[s, 1]
        out_ref[rows, 0, :] = jnp.where(core == 0, here, there)
        out_ref[rows, 1, :] = jnp.where(core == 0, there, here)

    for s in range(STREAMS):
        probe[s, :, :, 0:SIDE] = jnp.zeros((OWNERS, mo, SIDE), bf16)
        probe[s, :, :, SIDE:] = start_ref[s * m:(s + 1) * m, :].astype(bf16).reshape(OWNERS, mo, acts)
        nominal = jnp.where(core == 0, nominal_ref[0:1, :], nominal_ref[1:2, :])
        img[s] = nominal + base_ref[s * m:(s + 1) * m, :]
    tiles = tile_ref.shape[1]
    wide = half // tiles
    for tile in range(tiles):
        weight_ref[:, tile * wide:(tile + 1) * wide] = jnp.full(
            (1, wide), tile_ref[0, tile].astype(f32), f32
        )
    for ref in (field, direction, change, residual, gamma, rho, lost, owed):
        ref[...] = jnp.zeros_like(ref)
    lhs = probe[0, :, :, SIDE:].reshape(m, acts)
    for side in (1, 0):
        for i in range(BLOCKS):
            load(side, i).wait()
        part = lax.dot_general(
            lhs, jac[side], (((1,), (1,)), ((), ())), preferred_element_type=f32
        )
        if side == 1:
            ipart[0] = part.astype(bf16)
            core_sum(0).start()
            send_scalars(0, 0, [])
        else:
            qown[0] = part
    join_cores(0, 0)

    def turn(i, carry):
        for side in range(2):
            at = pl.multiple_of(i * block, block)
            jact[side, :, pl.ds(at, block)] = jac[side, pl.ds(at, block), :].T
        return carry

    lax.fori_loop(0, BLOCKS, turn, 0)

    def turn_half(t, carry):
        here, there = lax.rem(t + 1, 2), lax.rem(t, 2)
        k_here = (t + 1) // 2 - 1
        k_there = t // 2

        @pl.when(t >= 2)
        def _():
            join_cores(here, k_here)

        @pl.when(jnp.logical_and(t >= 2, t <= 2 * last + 1))
        def _():
            update(there, k_there - 1)

        @pl.when(t == 2 * last + 2)
        def _():
            finish(0)

        take_image(here, k_here)

        @pl.when(t <= 2 * last)
        def _():
            make_back(here)

        @pl.when(t > 2 * last)
        def _():
            send_kappa(here)

        @pl.when(t <= 2 * last + 1)
        def _():
            make_image(there, k_there)

        return carry

    lax.fori_loop(1, 2 * last + 3, turn_half, 0)
    finish(1)


def kernel_shards(nominal_field, sensitivity, aberrations, jacobian, tile_mask, regul, initial_commands):
    f32, bf16 = jnp.float32, jnp.bfloat16
    components, pixels, acts = jacobian.shape[1:]
    rows = components * pixels
    half = pixels
    reals = initial_commands.shape[0]
    n = lax.axis_size("section")
    m = reals // STREAMS
    mo = m // OWNERS
    core = lax.rem(lax.axis_index("section"), 2)
    mine = (jnp.arange(components) == core).astype(bf16)
    base = lax.dot_general(
        aberrations[:, :, None] * mine,
        sensitivity[0],
        (((1, 2), (0, 1)), ((), ())),
        preferred_element_type=f32,
    )
    vmem = pl.BlockSpec(memory_space=pltpu.VMEM)
    dma = pltpu.SemaphoreType.DMA
    commands, field = pl.pallas_call(
        functools.partial(control_kernel, n),
        out_shape=(
            jax.ShapeDtypeStruct((reals, acts), f32),
            jax.ShapeDtypeStruct((reals, components, pixels), f32),
        ),
        in_specs=[
            pl.BlockSpec(memory_space=pl.ANY),
            vmem,
            vmem,
            vmem,
            pl.BlockSpec(memory_space=pltpu.SMEM),
            vmem,
        ],
        out_specs=(vmem, vmem),
        scratch_shapes=[
            pltpu.VMEM((2, half, acts), bf16),
            pltpu.VMEM((2, acts, half), bf16),
            pltpu.VMEM((STREAMS, OWNERS, mo, SIDE + acts), bf16),
            pltpu.VMEM((STREAMS, OWNERS, mo, SIDE + acts), bf16),
            pltpu.VMEM((STREAMS, n - 1, mo, SIDE + acts), bf16),
            pltpu.VMEM((STREAMS, m, half), bf16),
            pltpu.VMEM((STREAMS, m, half), bf16),
            pltpu.VMEM((STREAMS, m, half), bf16),
            pltpu.VMEM((2, STREAMS, m, half), bf16),
            pltpu.VMEM((STREAMS, 2, m, half), bf16),
            pltpu.VMEM((STREAMS, m, half), f32),
            pltpu.VMEM((STREAMS, m, half), f32),
            pltpu.VMEM((STREAMS, m, half), f32),
            pltpu.VMEM((STREAMS, OWNERS, mo, acts), f32),
            pltpu.VMEM((STREAMS, OWNERS, mo, acts), f32),
            pltpu.VMEM((STREAMS, mo, acts), f32),
            pltpu.VMEM((m, max(2 * half, acts)), f32),
            pltpu.VMEM((STREAMS, OWNERS, mo, LANES), f32),
            pltpu.VMEM((STREAMS, OWNERS, mo, LANES), f32),
            pltpu.VMEM((n, 2, STREAMS, m, SIDE), bf16),
            pltpu.VMEM((STREAMS, 2, m, half), f32),
            pltpu.VMEM((STREAMS, OWNERS, mo, acts), f32),
            pltpu.VMEM((STREAMS, OWNERS, mo, acts), f32),
            pltpu.VMEM((STREAMS, OWNERS, mo, acts), bf16),
            pltpu.VMEM((STREAMS, n - 1, mo, acts), bf16),
            pltpu.VMEM((1, half), f32),
            pltpu.VMEM((2, n, STREAMS, m, LANES), f32),
            dma((2, BLOCKS)),
            dma((STREAMS,)),
            dma((STREAMS,)),
            dma((2, STREAMS)),
            dma((2, STREAMS)),
            dma((STREAMS,)),
            dma((STREAMS,)),
            dma((STREAMS, CHUNKS, OWNERS)),
            dma((STREAMS, CHUNKS, n - 1)),
            dma((STREAMS, CHUNKS, n - 1)),
            dma((STREAMS, CHUNKS, OWNERS)),
            dma((STREAMS, 2 * n - 1)),
            dma((STREAMS, 2 * n - 1)),
            dma((STREAMS, 2)),
            dma((STREAMS, 2)),
            dma((STREAMS, OWNERS)),
            dma((STREAMS, n - 1)),
            dma((2, STREAMS, n - 1)),
            dma((2, STREAMS, n - 1)),
        ],
        compiler_params=pltpu.CompilerParams(
            collective_id=0, has_side_effects=True, vmem_limit_bytes=48 * 1024 * 1024
        ),
        name="control_loop",
    )(
        jacobian.reshape(rows, acts),
        base,
        initial_commands,
        regul[None, :],
        tile_mask,
        nominal_field[0],
    )
    return commands, field.reshape(reals, 1, components, pixels)


def solution(mesh):
    placed = (
        P("wave", None, None),
        P("wave", None, None, None),
        P("groups", None),
        P("wave", None, None, "section"),
        P("wave", None),
        P("section"),
        P("groups", "section"),
    )

    def choose(*args):
        n, waves = mesh.shape["section"], mesh.shape["wave"]
        reals = args[6].shape[0]
        acts = args[3].shape[3]
        pixels = args[3].shape[2]
        fits = (
            n == 4
            and waves == 4
            and args[3].shape[1] == 2
            and reals % (16 * STREAMS * OWNERS) == 0
            and acts % (LANES * CHUNKS) == 0
            and pixels % (LANES * args[4].shape[1]) == 0
            and 2 * pixels * acts <= 2048 * 2048
            and reals <= 64
        )
        return (kernel_shards if fits else general_shards)(*args)

    return jax.shard_map(
        choose,
        mesh=mesh,
        in_specs=placed,
        out_specs=(P("groups", "section"), P("groups", "wave", None, None)),
        check_vma=False,
    )
```

```python
import functools

import jax
import jax.numpy as jnp
from jax import lax
from jax.experimental import pallas as pl
from jax.experimental.pallas import tpu as pltpu
from jax.sharding import PartitionSpec as P

ITERS = 2
CG = 5
LANES = 128
CHUNKS = 2
STREAMS = 2
OWNERS = 2
SIDE = 128
BLOCKS = 4
PAD = 128
FIRST = 7

epsilon = 1e-06


def to_section_image(command_bf, jac_block):
    partial_value = lax.dot_general(
        command_bf, jac_block, (((1,), (1,)), ((), ())), preferred_element_type=jnp.float32
    )
    return lax.psum_scatter(
        partial_value.astype(jnp.bfloat16), "section", scatter_dimension=1, tiled=True
    ).astype(jnp.float32)


def back_of(masked_share, jac_block):
    masked_bf = lax.all_gather(masked_share, "section", axis=1, tiled=True)
    partial_value = jnp.dot(masked_bf, jac_block, preferred_element_type=jnp.float32)
    owned = lax.psum_scatter(
        partial_value.astype(jnp.bfloat16), "wave", scatter_dimension=1, tiled=True
    ).astype(jnp.float32)
    return lax.all_gather(owned, "wave", axis=1, tiled=True)


def reduce_scalars(values):
    return lax.psum(values, "section")


def general_shards(nominal_field, sensitivity, aberrations, jacobian, tile_mask, regul, initial_commands):
    components = jacobian.shape[1]
    pixels = jacobian.shape[2]
    block_width = jacobian.shape[3]
    row_count = components * pixels
    share_rows = row_count // lax.axis_size("section")
    row_start = lax.axis_index("section") * share_rows
    jac_block = jacobian.reshape(row_count, block_width)
    tile_count = tile_mask.shape[1]
    weight_full = jnp.broadcast_to(
        tile_mask[0].astype(jnp.float32)[None, :, None],
        (components, tile_count, pixels // tile_count),
    ).reshape(1, row_count)
    weight = lax.dynamic_slice_in_dim(weight_full, row_start, share_rows, 1)
    mode_count = sensitivity.shape[1]
    sens_share = lax.dynamic_slice_in_dim(
        sensitivity.reshape(mode_count, row_count), row_start, share_rows, 1
    )
    nominal_share = lax.dynamic_slice_in_dim(
        nominal_field.reshape(1, row_count), row_start, share_rows, 1
    )
    field_now = nominal_share + jnp.dot(aberrations, sens_share, preferred_element_type=jnp.float32)
    commands = initial_commands
    field_now = field_now + to_section_image(commands.astype(jnp.bfloat16), jac_block)
    for iteration in range(ITERS):
        residual = -back_of((weight * field_now).astype(jnp.bfloat16), jac_block)
        direction = residual
        change = jnp.zeros_like(residual)
        field_step = jnp.zeros_like(field_now)
        norm_now = reduce_scalars(jnp.sum(residual * residual, axis=1))
        for inner_step in range(CG):
            image_now = to_section_image(direction.astype(jnp.bfloat16), jac_block)
            applied = (
                back_of((weight * image_now).astype(jnp.bfloat16), jac_block)
                + regul[None, :] * direction
            )
            curvature = reduce_scalars(jnp.sum(direction * applied, axis=1))
            step_len = norm_now / (curvature + epsilon)
            residual = residual - step_len[:, None] * applied
            norm_next = reduce_scalars(jnp.sum(residual * residual, axis=1))
            change = change + step_len[:, None] * direction
            field_step = field_step + step_len[:, None] * image_now
            direction = residual + (norm_next / (norm_now + epsilon))[:, None] * direction
            norm_now = norm_next
        commands = commands + change
        field_now = field_now + field_step
    whole_field = lax.all_gather(
        field_now.astype(jnp.bfloat16), "section", axis=1, tiled=True
    ).astype(field_now.dtype)
    return (commands, whole_field.reshape(whole_field.shape[0], 1, components, pixels))


def control_kernel(
    n,
    jac_hbm,
    base_ref,
    start_ref,
    regul_ref,
    tile_ref,
    nominal_ref,
    cmd_ref,
    out_ref,
    jac,
    jact,
    probe,
    wpart,
    wrecv,
    ipart,
    crecv,
    xsend,
    xrecv,
    masked,
    img,
    field,
    qown,
    direction,
    change,
    residual,
    acc,
    gamma,
    rho,
    kappas,
    other,
    lost,
    owed,
    opart,
    orecv,
    weight_ref,
    scal,
    jac_sem,
    cs_s,
    cs_r,
    xx_s,
    xx_r,
    cg_s,
    cg_r,
    ws_s,
    ws_r,
    ag_s,
    ag_r,
    fin_s,
    fin_r,
    out_s,
    out_r,
    ow_s,
    ow_r,
    sc_s,
    sc_r,
):
    f32, bf16 = jnp.float32, jnp.bfloat16
    half, acts = jac.shape[1:]
    mo = probe.shape[2]
    m = OWNERS * mo
    cut = [0, acts * FIRST // 16, acts]
    last = ITERS * CG
    sec, wav = lax.axis_index("section"), lax.axis_index("wave")
    core = lax.rem(sec, 2)
    sibling = {"section": sec + 1 - 2 * core}
    across = {"section": lax.rem(sec + 2, n)}
    first_owner = n // 2 - 1
    owners = [first_owner + o for o in range(OWNERS)]
    is_owner = jnp.logical_and(wav >= owners[0], wav <= owners[-1])
    far = jnp.where(wav <= first_owner, 1, 0)
    mine = jnp.clip(wav - first_owner, 0, OWNERS - 1)
    peers = range(n - 1)
    wav_peer = [{"wave": lax.rem(wav + k + 1, n)} for k in peers]

    block = half // BLOCKS

    def load(side, i):
        at = pl.multiple_of((core if side == 0 else 1 - core) * half + i * block, block)
        return pltpu.make_async_copy(
            jac_hbm.at[pl.ds(at, block)], jac.at[side, pl.ds(i * block, block)], jac_sem.at[side, i]
        )

    for side in (1, 0):
        for i in range(BLOCKS):
            load(side, i).start()
    barrier = pltpu.get_barrier_semaphore()
    slanted = [{"wave": lax.rem(wav + k + 1, n), **sibling} for k in peers]
    final_peer = slanted + wav_peer + [sibling]
    opposite = {"section": lax.rem(sec + 3 - 2 * core, n)}
    greeted = final_peer + [across, opposite]
    for p in greeted:
        pl.semaphore_signal(barrier, inc=1, device_id=p, device_id_type=pl.DeviceIdType.MESH)
    pl.semaphore_wait(barrier, len(greeted))

    def remote(src, dst, ss, rs, device):
        return pltpu.make_async_remote_copy(
            src_ref=src, dst_ref=dst, send_sem=ss, recv_sem=rs,
            device_id=device, device_id_type=pl.DeviceIdType.MESH,
        )

    def part_cols(c):
        low = 0 if c == 0 else SIDE + cut[c]
        return pl.ds(low, SIDE + cut[c + 1] - low)

    def core_sum(s):
        return remote(ipart.at[s], crecv.at[s], cs_s.at[s], cs_r.at[s], sibling)

    def x_sum(s, slot):
        return remote(xsend.at[s], xrecv.at[slot, s], xx_s.at[slot, s], xx_r.at[slot, s], across)

    def scal_copy(s, slot, k):
        return remote(
            scal.at[slot, sec, s],
            scal.at[slot, sec, s],
            sc_s.at[slot, s, k],
            sc_r.at[slot, s, k],
            {"section": lax.rem(sec + k + 1, n)},
        )

    def core_share(s):
        return remote(masked.at[s, 0], masked.at[s, 1], cg_s.at[s], cg_r.at[s], sibling)

    def to_owner(s, c, o):
        owner = first_owner + o
        k = lax.rem(wav - owner + n - 1 + n, n)
        return remote(
            wpart.at[s, o, :, part_cols(c)],
            wrecv.at[s, k, :, part_cols(c)],
            ws_s.at[s, c, o],
            ws_r.at[s, c, k],
            {"wave": owner},
        )

    def owed_copy(s, o):
        owner = first_owner + o
        k = lax.rem(wav - owner + n - 1 + n, n)
        return remote(
            opart.at[s, o], orecv.at[s, k], ow_s.at[s, o], ow_r.at[s, k], {"wave": owner}
        )

    def owed_at(s, k):
        return remote(opart.at[s, 0], orecv.at[s, k], ow_s.at[s, 0], ow_r.at[s, k], wav_peer[0])

    def at_owner(s, c, k):
        return remote(
            wpart.at[s, 0, :, part_cols(c)],
            wrecv.at[s, k, :, part_cols(c)],
            ws_s.at[s, c, 0],
            ws_r.at[s, c, k],
            wav_peer[0],
        )

    def from_owner(s, c, o, k):
        return remote(
            probe.at[s, o, :, part_cols(c)],
            probe.at[s, o, :, part_cols(c)],
            ag_s.at[s, c, k],
            ag_r.at[s, c, o],
            wav_peer[k],
        )

    def kappa_copy(s, k):
        return remote(
            kappas.at[wav, core, s],
            kappas.at[wav, core, s],
            fin_s.at[s, k],
            fin_r.at[s, k],
            final_peer[k],
        )

    def out_copy(s, at):
        return remote(
            (field, img)[at].at[s], other.at[s, at], out_s.at[s, at], out_r.at[s, at], sibling
        )

    def row_sum(values):
        return jnp.sum(values, axis=1, keepdims=True)

    def pack(values):
        lane = lax.broadcasted_iota(jnp.int32, (values[0].shape[0], SIDE), 1)
        packed = jnp.zeros(lane.shape, f32)
        for at, value in enumerate(values):
            rest = value
            for piece in range(3):
                top = rest.astype(bf16).astype(f32)
                rest = rest - top
                packed = jnp.where(lane == 3 * at + piece, top, packed)
        return packed.astype(bf16)

    def spread(column):
        return jnp.broadcast_to(column, (column.shape[0], LANES))

    def dot(lhs, rhs):
        padded = jnp.concatenate([lhs, jnp.zeros((PAD - m, lhs.shape[1]), bf16)], axis=0)
        return jnp.dot(padded, rhs, preferred_element_type=f32)[:m]

    def send_scalars(s, k, sums):
        lane = lax.broadcasted_iota(jnp.int32, (m, LANES), 1)
        packed = jnp.zeros((m, LANES), f32)
        for at, value in enumerate(sums):
            packed = jnp.where(lane == at, value, packed)
        slot = lax.rem(k, 2)
        scal[slot, sec, s] = packed
        for p in peers:
            scal_copy(s, slot, p).start()

    def make_image(s, k):
        def arrive(c):
            @pl.when(k > 0)
            def _():
                for o in range(OWNERS):
                    @pl.when(wav != owners[o])
                    def _():
                        from_owner(s, c, o, 0).wait_recv()

        def scalars(c, lhs):
            cols = slice(cut[c], cut[c + 1])
            wide = lhs.astype(f32)
            scaled = regul_ref[:, cols] * wide
            along = direction[s, :, :, cols].reshape(m, cut[c + 1] - cut[c])
            return [row_sum(wide * wide), row_sum(scaled * wide), row_sum(scaled * along)]

        sums = None
        for c in range(CHUNKS):
            arrive(c)
            lhs = probe[s, :, :, SIDE + cut[c]:SIDE + cut[c + 1]].reshape(m, cut[c + 1] - cut[c])
            for side in (1, 0):
                part = dot(lhs, jact[side, cut[c]:cut[c + 1], :])
                cols = slice(side * half, (side + 1) * half)
                if c:
                    part = acc[:, cols] + part
                if c < CHUNKS - 1:
                    acc[:, cols] = part
                elif side == 1:
                    ipart[s] = part.astype(bf16)
                    core_sum(s).start()
                else:
                    qown[s] = part
                if side == 1:
                    more = scalars(c, lhs)
                    sums = more if sums is None else [x + y for x, y in zip(sums, more)]
                    if c == CHUNKS - 1:
                        send_scalars(s, k, sums)
        step = row_sum(probe[s, :, :, 0:SIDE].reshape(m, SIDE).astype(f32))
        field[s] = field[s] + step * img[s]
        step = step.reshape(OWNERS, mo, 1)
        change[s] = change[s] + step * direction[s]
        owed[s] = owed[s] + step * lost[s]

    def settle(s):
        for p in peers:
            owed_at(s, p).wait_recv()
        total = opart[s, mine].astype(f32)
        for p in peers:
            total = total + orecv[s, p].astype(f32)
        residual[s] = residual[s] - total

    def join_cores(s, k):
        core_sum(s).wait()
        xsend[s] = (qown[s] + crecv[s].astype(f32)).astype(bf16)
        x_sum(s, lax.rem(k, 2)).start()

        @pl.when(k == CG)
        def _():
            opart[s] = owed[s].astype(bf16)

    def take_image(s, k):
        slot = lax.rem(k, 2)
        for p in peers:
            scal_copy(s, slot, p).wait()
        lanes = scal[slot, 0, s]
        for at in range(1, n):
            lanes = lanes + scal[slot, at, s]
        norm, aa, bb = [lanes[:, at:at + 1] for at in range(3)]
        norm_before = gamma[s].reshape(m, LANES)[:, 0:1]
        rho_before = rho[s].reshape(m, LANES)[:, 0:1]
        ratio = norm / (norm_before + epsilon)
        ratio = jnp.where(lax.rem(k, CG) == 1, 0.0, ratio)
        ratio = jnp.where(k == 0, 1.0, ratio)
        rho_now = jnp.maximum(aa + 2.0 * ratio * bb + ratio * ratio * rho_before, 0.0)
        gamma[s] = spread(norm).reshape(OWNERS, mo, LANES)
        rho[s] = spread(rho_now).reshape(OWNERS, mo, LANES)
        fresh = jnp.where(k == 0, 0.0, 1.0)
        direction[s] = (
            fresh * probe[s, :, :, SIDE:].astype(f32) + ratio.reshape(OWNERS, mo, 1) * direction[s]
        )
        img[s] = ratio * img[s]
        @pl.when(k > 0)
        def _():
            for c in range(CHUNKS):
                to_owner(s, c, far).wait_send()

                @pl.when(jnp.logical_not(is_owner))
                def _():
                    to_owner(s, c, 1 - far).wait_send()

            @pl.when(is_owner)
            def _():
                for c in range(CHUNKS):
                    for p in peers:
                        from_owner(s, c, mine, p).wait_send()

            @pl.when(k == CG + 1)
            def _():
                owed_copy(s, far).wait_send()

                @pl.when(jnp.logical_not(is_owner))
                def _():
                    owed_copy(s, 1 - far).wait_send()

        x_sum(s, slot).wait()
        now = xsend[s].astype(f32) + xrecv[slot, s].astype(f32) + img[s]
        img[s] = now
        kept = (weight_ref[...] * now).astype(bf16)
        masked[s, 0] = kept

        @pl.when(k < last)
        def _():
            core_share(s).start()

        @pl.when(k == CG)
        def _():
            owed_copy(s, far).start()

            @pl.when(jnp.logical_not(is_owner))
            def _():
                owed_copy(s, 1 - far).start()

    def square(s, side):
        wide = masked[s, side].astype(f32)
        return row_sum(wide * wide)

    def make_back(s):
        lhs = masked[s, 0]
        for c in range(CHUNKS):
            cols = slice(cut[c], cut[c + 1])
            acc[:, cols] = dot(lhs, jac[0, :, cols])
        kappa = square(s, 0)
        core_share(s).wait()
        kappa = pack([kappa + square(s, 1)])
        wpart[s, :, :, 0:SIDE] = kappa.reshape(OWNERS, mo, SIDE)
        lhs = masked[s, 1]
        for c in range(CHUNKS):
            cols = slice(cut[c], cut[c + 1])
            part = acc[:, cols] + dot(lhs, jac[1, :, cols])
            sent = part.astype(bf16)
            wpart[s, :, :, SIDE + cut[c]:SIDE + cut[c + 1]] = sent.reshape(OWNERS, mo, cut[c + 1] - cut[c])
            to_owner(s, c, far).start()

            @pl.when(jnp.logical_not(is_owner))
            def _():
                to_owner(s, c, 1 - far).start()

            lost[s, :, :, cols] = (part - sent.astype(f32)).reshape(OWNERS, mo, cut[c + 1] - cut[c])

    def update(s, k):
        @pl.when(is_owner)
        def _():
            again = jnp.where(k == CG, 1.0, 0.0)

            @pl.when(k == CG)
            def _():
                settle(s)

            for c in range(CHUNKS):
                for p in peers:
                    at_owner(s, c, p).wait_recv()
                if c == 0:
                    kappa = wpart[s, mine, :, 0:SIDE].astype(f32)
                    for p in peers:
                        kappa = kappa + wrecv[s, p, :, 0:SIDE].astype(f32)
                    kappa = row_sum(kappa)
                    norm, rho_now = gamma[s, mine][:, 0:1], rho[s, mine][:, 0:1]
                    step = norm / (kappa + rho_now + epsilon)
                    step = jnp.where(k == 0, 1.0, step)
                    probe[s, mine, :, 0:SIDE] = pack([step])
                cols = slice(cut[c], cut[c + 1])
                wide = slice(SIDE + cut[c], SIDE + cut[c + 1])
                total = wpart[s, mine, :, wide].astype(f32)
                for p in peers:
                    total = total + wrecv[s, p, :, wide].astype(f32)
                along = direction[s, mine, :, cols]
                weight = regul_ref[:, cols]
                after = residual[s, :, cols] - step * (total + weight * along)
                after = after + again * (weight * (change[s, mine, :, cols] + step * along))
                residual[s, :, cols] = after
                probe[s, mine, :, wide] = after.astype(bf16)
                for p in (1, 0, 2):
                    from_owner(s, c, mine, p).start()

    def send_kappa(s):
        for at in range(2):
            out_copy(s, at).start()
        kappas[wav, core, s] = pack([square(s, 0)])
        for p in range(len(final_peer)):
            kappa_copy(s, p).start()

    def finish(s):
        for p in range(len(final_peer)):
            kappa_copy(s, p).wait()
        kappa = jnp.zeros((m, SIDE), f32)
        for w in range(n):
            for c in range(2):
                kappa = kappa + kappas[w, c, s].astype(f32)
        step = gamma[s].reshape(m, LANES)[:, 0:1]
        step = step / (row_sum(kappa) + rho[s].reshape(m, LANES)[:, 0:1] + epsilon)
        rows = pl.ds(s * m, m)
        moved = change[s] + step.reshape(OWNERS, mo, 1) * direction[s]
        cmd_ref[rows, :] = start_ref[rows, :] + moved.reshape(m, acts)
        for at in range(2):
            out_copy(s, at).wait()
        here = field[s] + step * img[s]
        there = other[s, 0] + step * other[s, 1]
        out_ref[rows, 0, :] = jnp.where(core == 0, here, there)
        out_ref[rows, 1, :] = jnp.where(core == 0, there, here)

    for s in range(STREAMS):
        probe[s, :, :, 0:SIDE] = jnp.zeros((OWNERS, mo, SIDE), bf16)
        probe[s, :, :, SIDE:] = start_ref[s * m:(s + 1) * m, :].astype(bf16).reshape(OWNERS, mo, acts)
        nominal = jnp.where(core == 0, nominal_ref[0:1, :], nominal_ref[1:2, :])
        img[s] = nominal + base_ref[s * m:(s + 1) * m, :]
    tiles = tile_ref.shape[1]
    wide = half // tiles
    for tile in range(tiles):
        weight_ref[:, tile * wide:(tile + 1) * wide] = jnp.full(
            (1, wide), tile_ref[0, tile].astype(f32), f32
        )
    for ref in (field, direction, change, residual, gamma, rho, lost, owed):
        ref[...] = jnp.zeros_like(ref)
    lhs = probe[0, :, :, SIDE:].reshape(m, acts)
    for side in (1, 0):
        for i in range(BLOCKS):
            load(side, i).wait()
        part = lax.dot_general(
            lhs, jac[side], (((1,), (1,)), ((), ())), preferred_element_type=f32
        )
        if side == 1:
            ipart[0] = part.astype(bf16)
            core_sum(0).start()
            send_scalars(0, 0, [])
        else:
            qown[0] = part
    join_cores(0, 0)

    def turn(i, carry):
        for side in range(2):
            at = pl.multiple_of(i * block, block)
            jact[side, :, pl.ds(at, block)] = jac[side, pl.ds(at, block), :].T
        return carry

    lax.fori_loop(0, BLOCKS, turn, 0)

    def turn_half(t, carry):
        here, there = lax.rem(t + 1, 2), lax.rem(t, 2)
        k_here = (t + 1) // 2 - 1
        k_there = t // 2

        @pl.when(t >= 2)
        def _():
            join_cores(here, k_here)

        @pl.when(jnp.logical_and(t >= 2, t <= 2 * last + 1))
        def _():
            update(there, k_there - 1)

        @pl.when(t == 2 * last + 2)
        def _():
            finish(0)

        take_image(here, k_here)

        @pl.when(t <= 2 * last)
        def _():
            make_back(here)

        @pl.when(t > 2 * last)
        def _():
            send_kappa(here)

        @pl.when(t <= 2 * last + 1)
        def _():
            make_image(there, k_there)

        return carry

    lax.fori_loop(1, 2 * last + 3, turn_half, 0)
    finish(1)


def kernel_shards(nominal_field, sensitivity, aberrations, jacobian, tile_mask, regul, initial_commands):
    f32, bf16 = jnp.float32, jnp.bfloat16
    components, pixels, acts = jacobian.shape[1:]
    rows = components * pixels
    half = pixels
    reals = initial_commands.shape[0]
    n = lax.axis_size("section")
    m = reals // STREAMS
    mo = m // OWNERS
    core = lax.rem(lax.axis_index("section"), 2)
    mine = (jnp.arange(components) == core).astype(bf16)
    base = lax.dot_general(
        aberrations[:, :, None] * mine,
        sensitivity[0],
        (((1, 2), (0, 1)), ((), ())),
        preferred_element_type=f32,
    )
    vmem = pl.BlockSpec(memory_space=pltpu.VMEM)
    dma = pltpu.SemaphoreType.DMA
    commands, field = pl.pallas_call(
        functools.partial(control_kernel, n),
        out_shape=(
            jax.ShapeDtypeStruct((reals, acts), f32),
            jax.ShapeDtypeStruct((reals, components, pixels), f32),
        ),
        in_specs=[
            pl.BlockSpec(memory_space=pl.ANY),
            vmem,
            vmem,
            vmem,
            pl.BlockSpec(memory_space=pltpu.SMEM),
            vmem,
        ],
        out_specs=(vmem, vmem),
        scratch_shapes=[
            pltpu.VMEM((2, half, acts), bf16),
            pltpu.VMEM((2, acts, half), bf16),
            pltpu.VMEM((STREAMS, OWNERS, mo, SIDE + acts), bf16),
            pltpu.VMEM((STREAMS, OWNERS, mo, SIDE + acts), bf16),
            pltpu.VMEM((STREAMS, n - 1, mo, SIDE + acts), bf16),
            pltpu.VMEM((STREAMS, m, half), bf16),
            pltpu.VMEM((STREAMS, m, half), bf16),
            pltpu.VMEM((STREAMS, m, half), bf16),
            pltpu.VMEM((2, STREAMS, m, half), bf16),
            pltpu.VMEM((STREAMS, 2, m, half), bf16),
            pltpu.VMEM((STREAMS, m, half), f32),
            pltpu.VMEM((STREAMS, m, half), f32),
            pltpu.VMEM((STREAMS, m, half), f32),
            pltpu.VMEM((STREAMS, OWNERS, mo, acts), f32),
            pltpu.VMEM((STREAMS, OWNERS, mo, acts), f32),
            pltpu.VMEM((STREAMS, mo, acts), f32),
            pltpu.VMEM((m, max(2 * half, acts)), f32),
            pltpu.VMEM((STREAMS, OWNERS, mo, LANES), f32),
            pltpu.VMEM((STREAMS, OWNERS, mo, LANES), f32),
            pltpu.VMEM((n, 2, STREAMS, m, SIDE), bf16),
            pltpu.VMEM((STREAMS, 2, m, half), f32),
            pltpu.VMEM((STREAMS, OWNERS, mo, acts), f32),
            pltpu.VMEM((STREAMS, OWNERS, mo, acts), f32),
            pltpu.VMEM((STREAMS, OWNERS, mo, acts), bf16),
            pltpu.VMEM((STREAMS, n - 1, mo, acts), bf16),
            pltpu.VMEM((1, half), f32),
            pltpu.VMEM((2, n, STREAMS, m, LANES), f32),
            dma((2, BLOCKS)),
            dma((STREAMS,)),
            dma((STREAMS,)),
            dma((2, STREAMS)),
            dma((2, STREAMS)),
            dma((STREAMS,)),
            dma((STREAMS,)),
            dma((STREAMS, CHUNKS, OWNERS)),
            dma((STREAMS, CHUNKS, n - 1)),
            dma((STREAMS, CHUNKS, n - 1)),
            dma((STREAMS, CHUNKS, OWNERS)),
            dma((STREAMS, 2 * n - 1)),
            dma((STREAMS, 2 * n - 1)),
            dma((STREAMS, 2)),
            dma((STREAMS, 2)),
            dma((STREAMS, OWNERS)),
            dma((STREAMS, n - 1)),
            dma((2, STREAMS, n - 1)),
            dma((2, STREAMS, n - 1)),
        ],
        compiler_params=pltpu.CompilerParams(
            collective_id=0, has_side_effects=True, vmem_limit_bytes=48 * 1024 * 1024
        ),
        name="control_loop",
    )(
        jacobian.reshape(rows, acts),
        base,
        initial_commands,
        regul[None, :],
        tile_mask,
        nominal_field[0],
    )
    return commands, field.reshape(reals, 1, components, pixels)


def solution(mesh):
    placed = (
        P("wave", None, None),
        P("wave", None, None, None),
        P("groups", None),
        P("wave", None, None, "section"),
        P("wave", None),
        P("section"),
        P("groups", "section"),
    )

    def choose(*args):
        n, waves = mesh.shape["section"], mesh.shape["wave"]
        reals = args[6].shape[0]
        acts = args[3].shape[3]
        pixels = args[3].shape[2]
        fits = (
            n == 4
            and waves == 4
            and args[3].shape[1] == 2
            and reals % (16 * STREAMS * OWNERS) == 0
            and acts % (LANES * 16) == 0
            and pixels % (LANES * args[4].shape[1]) == 0
            and 2 * pixels * acts <= 2048 * 2048
            and reals <= 64
        )
        return (kernel_shards if fits else general_shards)(*args)

    return jax.shard_map(
        choose,
        mesh=mesh,
        in_specs=placed,
        out_specs=(P("groups", "section"), P("groups", "wave", None, None)),
        check_vma=False,
    )
```

```python
import functools

import jax
import jax.numpy as jnp
from jax import lax
from jax.experimental import pallas as pl
from jax.experimental.pallas import tpu as pltpu
from jax.sharding import PartitionSpec as P

ITERS = 2
CG = 5
LANES = 128
CHUNKS = 2
STREAMS = 2
OWNERS = 2
SIDE = 128
BLOCKS = 4
PAD = 128
FIRST = 7

epsilon = 1e-06


def to_section_image(command_bf, jac_block):
    partial_value = lax.dot_general(
        command_bf, jac_block, (((1,), (1,)), ((), ())), preferred_element_type=jnp.float32
    )
    return lax.psum_scatter(
        partial_value.astype(jnp.bfloat16), "section", scatter_dimension=1, tiled=True
    ).astype(jnp.float32)


def back_of(masked_share, jac_block):
    masked_bf = lax.all_gather(masked_share, "section", axis=1, tiled=True)
    partial_value = jnp.dot(masked_bf, jac_block, preferred_element_type=jnp.float32)
    owned = lax.psum_scatter(
        partial_value.astype(jnp.bfloat16), "wave", scatter_dimension=1, tiled=True
    ).astype(jnp.float32)
    return lax.all_gather(owned, "wave", axis=1, tiled=True)


def reduce_scalars(values):
    return lax.psum(values, "section")


def general_shards(nominal_field, sensitivity, aberrations, jacobian, tile_mask, regul, initial_commands):
    components = jacobian.shape[1]
    pixels = jacobian.shape[2]
    block_width = jacobian.shape[3]
    row_count = components * pixels
    share_rows = row_count // lax.axis_size("section")
    row_start = lax.axis_index("section") * share_rows
    jac_block = jacobian.reshape(row_count, block_width)
    tile_count = tile_mask.shape[1]
    weight_full = jnp.broadcast_to(
        tile_mask[0].astype(jnp.float32)[None, :, None],
        (components, tile_count, pixels // tile_count),
    ).reshape(1, row_count)
    weight = lax.dynamic_slice_in_dim(weight_full, row_start, share_rows, 1)
    mode_count = sensitivity.shape[1]
    sens_share = lax.dynamic_slice_in_dim(
        sensitivity.reshape(mode_count, row_count), row_start, share_rows, 1
    )
    nominal_share = lax.dynamic_slice_in_dim(
        nominal_field.reshape(1, row_count), row_start, share_rows, 1
    )
    field_now = nominal_share + jnp.dot(aberrations, sens_share, preferred_element_type=jnp.float32)
    commands = initial_commands
    field_now = field_now + to_section_image(commands.astype(jnp.bfloat16), jac_block)
    for iteration in range(ITERS):
        residual = -back_of((weight * field_now).astype(jnp.bfloat16), jac_block)
        direction = residual
        change = jnp.zeros_like(residual)
        field_step = jnp.zeros_like(field_now)
        norm_now = reduce_scalars(jnp.sum(residual * residual, axis=1))
        for inner_step in range(CG):
            image_now = to_section_image(direction.astype(jnp.bfloat16), jac_block)
            applied = (
                back_of((weight * image_now).astype(jnp.bfloat16), jac_block)
                + regul[None, :] * direction
            )
            curvature = reduce_scalars(jnp.sum(direction * applied, axis=1))
            step_len = norm_now / (curvature + epsilon)
            residual = residual - step_len[:, None] * applied
            norm_next = reduce_scalars(jnp.sum(residual * residual, axis=1))
            change = change + step_len[:, None] * direction
            field_step = field_step + step_len[:, None] * image_now
            direction = residual + (norm_next / (norm_now + epsilon))[:, None] * direction
            norm_now = norm_next
        commands = commands + change
        field_now = field_now + field_step
    whole_field = lax.all_gather(
        field_now.astype(jnp.bfloat16), "section", axis=1, tiled=True
    ).astype(field_now.dtype)
    return (commands, whole_field.reshape(whole_field.shape[0], 1, components, pixels))


def control_kernel(
    n,
    jac_hbm,
    base_ref,
    start_ref,
    regul_ref,
    tile_ref,
    nominal_ref,
    cmd_ref,
    out_ref,
    jac,
    jact,
    probe,
    wpart,
    wrecv,
    ipart,
    crecv,
    xsend,
    xrecv,
    masked,
    img,
    field,
    qown,
    direction,
    change,
    residual,
    acc,
    gamma,
    rho,
    kappas,
    other,
    lost,
    owed,
    opart,
    orecv,
    weight_ref,
    scal,
    jac_sem,
    cs_s,
    cs_r,
    xx_s,
    xx_r,
    cg_s,
    cg_r,
    ws_s,
    ws_r,
    ag_s,
    ag_r,
    fin_s,
    fin_r,
    out_s,
    out_r,
    ow_s,
    ow_r,
    sc_s,
    sc_r,
):
    f32, bf16 = jnp.float32, jnp.bfloat16
    half, acts = jac.shape[1:]
    mo = probe.shape[2]
    m = OWNERS * mo
    cut = [0, acts * FIRST // 16, acts]
    last = ITERS * CG
    sec, wav = lax.axis_index("section"), lax.axis_index("wave")
    core = lax.rem(sec, 2)
    sibling = {"section": sec + 1 - 2 * core}
    across = {"section": lax.rem(sec + 2, n)}
    first_owner = n // 2 - 1
    owners = [first_owner + o for o in range(OWNERS)]
    is_owner = jnp.logical_and(wav >= owners[0], wav <= owners[-1])
    far = jnp.where(wav <= first_owner, 1, 0)
    mine = jnp.clip(wav - first_owner, 0, OWNERS - 1)
    peers = range(n - 1)
    wav_peer = [{"wave": lax.rem(wav + k + 1, n)} for k in peers]

    block = half // BLOCKS

    def load(side, i):
        at = pl.multiple_of((core if side == 0 else 1 - core) * half + i * block, block)
        return pltpu.make_async_copy(
            jac_hbm.at[pl.ds(at, block)], jac.at[side, pl.ds(i * block, block)], jac_sem.at[side, i]
        )

    for side in (1, 0):
        for i in range(BLOCKS):
            load(side, i).start()
    barrier = pltpu.get_barrier_semaphore()
    slanted = [{"wave": lax.rem(wav + k + 1, n), **sibling} for k in peers]
    final_peer = slanted + wav_peer + [sibling]
    opposite = {"section": lax.rem(sec + 3 - 2 * core, n)}
    greeted = final_peer + [across, opposite]
    for p in greeted:
        pl.semaphore_signal(barrier, inc=1, device_id=p, device_id_type=pl.DeviceIdType.MESH)
    pl.semaphore_wait(barrier, len(greeted))

    def remote(src, dst, ss, rs, device):
        return pltpu.make_async_remote_copy(
            src_ref=src, dst_ref=dst, send_sem=ss, recv_sem=rs,
            device_id=device, device_id_type=pl.DeviceIdType.MESH,
        )

    def part_cols(c):
        low = 0 if c == 0 else SIDE + cut[c]
        return pl.ds(low, SIDE + cut[c + 1] - low)

    def core_sum(s):
        return remote(ipart.at[s], crecv.at[s], cs_s.at[s], cs_r.at[s], sibling)

    def x_sum(s, slot):
        return remote(xsend.at[s], xrecv.at[slot, s], xx_s.at[slot, s], xx_r.at[slot, s], across)

    def scal_copy(s, slot, k):
        return remote(
            scal.at[slot, sec, s],
            scal.at[slot, sec, s],
            sc_s.at[slot, s, k],
            sc_r.at[slot, s, k],
            {"section": lax.rem(sec + k + 1, n)},
        )

    def core_share(s):
        return remote(masked.at[s, 0], masked.at[s, 1], cg_s.at[s], cg_r.at[s], sibling)

    def to_owner(s, c, o):
        owner = first_owner + o
        k = lax.rem(wav - owner + n - 1 + n, n)
        return remote(
            wpart.at[s, o, :, part_cols(c)],
            wrecv.at[s, k, :, part_cols(c)],
            ws_s.at[s, c, o],
            ws_r.at[s, c, k],
            {"wave": owner},
        )

    def owed_copy(s, o):
        owner = first_owner + o
        k = lax.rem(wav - owner + n - 1 + n, n)
        return remote(
            opart.at[s, o], orecv.at[s, k], ow_s.at[s, o], ow_r.at[s, k], {"wave": owner}
        )

    def owed_at(s, k):
        return remote(opart.at[s, 0], orecv.at[s, k], ow_s.at[s, 0], ow_r.at[s, k], wav_peer[0])

    def at_owner(s, c, k):
        return remote(
            wpart.at[s, 0, :, part_cols(c)],
            wrecv.at[s, k, :, part_cols(c)],
            ws_s.at[s, c, 0],
            ws_r.at[s, c, k],
            wav_peer[0],
        )

    def from_owner(s, c, o, k):
        return remote(
            probe.at[s, o, :, part_cols(c)],
            probe.at[s, o, :, part_cols(c)],
            ag_s.at[s, c, k],
            ag_r.at[s, c, o],
            wav_peer[k],
        )

    def kappa_copy(s, k):
        return remote(
            kappas.at[wav, core, s],
            kappas.at[wav, core, s],
            fin_s.at[s, k],
            fin_r.at[s, k],
            final_peer[k],
        )

    def out_copy(s, at):
        return remote(
            (field, img)[at].at[s], other.at[s, at], out_s.at[s, at], out_r.at[s, at], sibling
        )

    def row_sum(values):
        return jnp.sum(values, axis=1, keepdims=True)

    def pack(values):
        lane = lax.broadcasted_iota(jnp.int32, (values[0].shape[0], SIDE), 1)
        packed = jnp.zeros(lane.shape, f32)
        for at, value in enumerate(values):
            rest = value
            for piece in range(3):
                top = rest.astype(bf16).astype(f32)
                rest = rest - top
                packed = jnp.where(lane == 3 * at + piece, top, packed)
        return packed.astype(bf16)

    def spread(column):
        return jnp.broadcast_to(column, (column.shape[0], LANES))

    def dot(lhs, rhs):
        padded = jnp.concatenate([lhs, jnp.zeros((PAD - m, lhs.shape[1]), bf16)], axis=0)
        return jnp.dot(padded, rhs, preferred_element_type=f32)[:m]

    def send_scalars(s, k, sums):
        lane = lax.broadcasted_iota(jnp.int32, (m, LANES), 1)
        packed = jnp.zeros((m, LANES), f32)
        for at, value in enumerate(sums):
            packed = jnp.where(lane == at, value, packed)
        slot = lax.rem(k, 2)
        scal[slot, sec, s] = packed
        for p in peers:
            scal_copy(s, slot, p).start()

    def make_image(s, k):
        def arrive(c):
            @pl.when(k > 0)
            def _():
                for o in range(OWNERS):
                    @pl.when(wav != owners[o])
                    def _():
                        from_owner(s, c, o, 0).wait_recv()

        def scalars(c, lhs):
            cols = slice(cut[c], cut[c + 1])
            wide = lhs.astype(f32)
            scaled = regul_ref[:, cols] * wide
            along = direction[s, :, :, cols].reshape(m, cut[c + 1] - cut[c])
            return [row_sum(wide * wide), row_sum(scaled * wide), row_sum(scaled * along)]

        sums = None
        for c in range(CHUNKS):
            arrive(c)
            lhs = probe[s, :, :, SIDE + cut[c]:SIDE + cut[c + 1]].reshape(m, cut[c + 1] - cut[c])
            for side in (1, 0):
                part = dot(lhs, jact[side, cut[c]:cut[c + 1], :])
                cols = slice(side * half, (side + 1) * half)
                if c:
                    part = acc[:, cols] + part
                if c < CHUNKS - 1:
                    acc[:, cols] = part
                elif side == 1:
                    ipart[s] = part.astype(bf16)
                    core_sum(s).start()
                else:
                    qown[s] = part
                if side == 1:
                    more = scalars(c, lhs)
                    sums = more if sums is None else [x + y for x, y in zip(sums, more)]
                    if c == CHUNKS - 1:
                        send_scalars(s, k, sums)

    def settle(s):
        for p in peers:
            owed_at(s, p).wait_recv()
        total = opart[s, mine].astype(f32)
        for p in peers:
            total = total + orecv[s, p].astype(f32)
        residual[s] = residual[s] - total

    def settle_step(s):
        step = row_sum(probe[s, :, :, 0:SIDE].reshape(m, SIDE).astype(f32))
        field[s] = field[s] + step * img[s]
        step = step.reshape(OWNERS, mo, 1)
        change[s] = change[s] + step * direction[s]
        owed[s] = owed[s] + step * lost[s]

    def join_cores(s, k):
        core_sum(s).wait()
        xsend[s] = (qown[s] + crecv[s].astype(f32)).astype(bf16)
        x_sum(s, lax.rem(k, 2)).start()

        @pl.when(k == CG)
        def _():
            opart[s] = owed[s].astype(bf16)

    def take_image(s, k):
        slot = lax.rem(k, 2)
        for p in peers:
            scal_copy(s, slot, p).wait()
        lanes = scal[slot, 0, s]
        for at in range(1, n):
            lanes = lanes + scal[slot, at, s]
        norm, aa, bb = [lanes[:, at:at + 1] for at in range(3)]
        norm_before = gamma[s].reshape(m, LANES)[:, 0:1]
        rho_before = rho[s].reshape(m, LANES)[:, 0:1]
        ratio = norm / (norm_before + epsilon)
        ratio = jnp.where(lax.rem(k, CG) == 1, 0.0, ratio)
        ratio = jnp.where(k == 0, 1.0, ratio)
        rho_now = jnp.maximum(aa + 2.0 * ratio * bb + ratio * ratio * rho_before, 0.0)
        gamma[s] = spread(norm).reshape(OWNERS, mo, LANES)
        rho[s] = spread(rho_now).reshape(OWNERS, mo, LANES)
        fresh = jnp.where(k == 0, 0.0, 1.0)
        direction[s] = (
            fresh * probe[s, :, :, SIDE:].astype(f32) + ratio.reshape(OWNERS, mo, 1) * direction[s]
        )
        img[s] = ratio * img[s]
        @pl.when(k > 0)
        def _():
            for c in range(CHUNKS):
                to_owner(s, c, far).wait_send()

                @pl.when(jnp.logical_not(is_owner))
                def _():
                    to_owner(s, c, 1 - far).wait_send()

            @pl.when(is_owner)
            def _():
                for c in range(CHUNKS):
                    for p in peers:
                        from_owner(s, c, mine, p).wait_send()

            @pl.when(k == CG + 1)
            def _():
                owed_copy(s, far).wait_send()

                @pl.when(jnp.logical_not(is_owner))
                def _():
                    owed_copy(s, 1 - far).wait_send()

        x_sum(s, slot).wait()
        now = xsend[s].astype(f32) + xrecv[slot, s].astype(f32) + img[s]
        img[s] = now
        kept = (weight_ref[...] * now).astype(bf16)
        masked[s, 0] = kept

        @pl.when(k < last)
        def _():
            core_share(s).start()

        @pl.when(k == CG)
        def _():
            owed_copy(s, far).start()

            @pl.when(jnp.logical_not(is_owner))
            def _():
                owed_copy(s, 1 - far).start()

    def square(s, side):
        wide = masked[s, side].astype(f32)
        return row_sum(wide * wide)

    def make_back(s):
        lhs = masked[s, 0]
        for c in range(CHUNKS):
            cols = slice(cut[c], cut[c + 1])
            acc[:, cols] = dot(lhs, jac[0, :, cols])
        kappa = square(s, 0)
        core_share(s).wait()
        kappa = pack([kappa + square(s, 1)])
        wpart[s, :, :, 0:SIDE] = kappa.reshape(OWNERS, mo, SIDE)
        lhs = masked[s, 1]
        for c in range(CHUNKS):
            cols = slice(cut[c], cut[c + 1])
            part = acc[:, cols] + dot(lhs, jac[1, :, cols])
            sent = part.astype(bf16)
            wpart[s, :, :, SIDE + cut[c]:SIDE + cut[c + 1]] = sent.reshape(OWNERS, mo, cut[c + 1] - cut[c])
            to_owner(s, c, far).start()

            @pl.when(jnp.logical_not(is_owner))
            def _():
                to_owner(s, c, 1 - far).start()

            acc[:, cols] = part

        lost[s] = acc[:, 0:acts].reshape(OWNERS, mo, acts) - wpart[s, :, :, SIDE:].astype(f32)

    def update(s, k):
        @pl.when(is_owner)
        def _():
            again = jnp.where(k == CG, 1.0, 0.0)

            @pl.when(k == CG)
            def _():
                settle(s)

            for c in range(CHUNKS):
                for p in peers:
                    at_owner(s, c, p).wait_recv()
                if c == 0:
                    kappa = wpart[s, mine, :, 0:SIDE].astype(f32)
                    for p in peers:
                        kappa = kappa + wrecv[s, p, :, 0:SIDE].astype(f32)
                    kappa = row_sum(kappa)
                    norm, rho_now = gamma[s, mine][:, 0:1], rho[s, mine][:, 0:1]
                    step = norm / (kappa + rho_now + epsilon)
                    step = jnp.where(k == 0, 1.0, step)
                    probe[s, mine, :, 0:SIDE] = pack([step])
                cols = slice(cut[c], cut[c + 1])
                wide = slice(SIDE + cut[c], SIDE + cut[c + 1])
                total = wpart[s, mine, :, wide].astype(f32)
                for p in peers:
                    total = total + wrecv[s, p, :, wide].astype(f32)
                along = direction[s, mine, :, cols]
                weight = regul_ref[:, cols]
                after = residual[s, :, cols] - step * (total + weight * along)
                after = after + again * (weight * (change[s, mine, :, cols] + step * along))
                residual[s, :, cols] = after
                probe[s, mine, :, wide] = after.astype(bf16)
                for p in (1, 0, 2):
                    from_owner(s, c, mine, p).start()

    def send_kappa(s):
        for at in range(2):
            out_copy(s, at).start()
        kappas[wav, core, s] = pack([square(s, 0)])
        for p in range(len(final_peer)):
            kappa_copy(s, p).start()

    def finish(s):
        for p in range(len(final_peer)):
            kappa_copy(s, p).wait()
        kappa = jnp.zeros((m, SIDE), f32)
        for w in range(n):
            for c in range(2):
                kappa = kappa + kappas[w, c, s].astype(f32)
        step = gamma[s].reshape(m, LANES)[:, 0:1]
        step = step / (row_sum(kappa) + rho[s].reshape(m, LANES)[:, 0:1] + epsilon)
        rows = pl.ds(s * m, m)
        moved = change[s] + step.reshape(OWNERS, mo, 1) * direction[s]
        cmd_ref[rows, :] = start_ref[rows, :] + moved.reshape(m, acts)
        for at in range(2):
            out_copy(s, at).wait()
        here = field[s] + step * img[s]
        there = other[s, 0] + step * other[s, 1]
        out_ref[rows, 0, :] = jnp.where(core == 0, here, there)
        out_ref[rows, 1, :] = jnp.where(core == 0, there, here)

    for s in range(STREAMS):
        probe[s, :, :, 0:SIDE] = jnp.zeros((OWNERS, mo, SIDE), bf16)
        probe[s, :, :, SIDE:] = start_ref[s * m:(s + 1) * m, :].astype(bf16).reshape(OWNERS, mo, acts)
        nominal = jnp.where(core == 0, nominal_ref[0:1, :], nominal_ref[1:2, :])
        img[s] = nominal + base_ref[s * m:(s + 1) * m, :]
    tiles = tile_ref.shape[1]
    wide = half // tiles
    for tile in range(tiles):
        weight_ref[:, tile * wide:(tile + 1) * wide] = jnp.full(
            (1, wide), tile_ref[0, tile].astype(f32), f32
        )
    for ref in (field, direction, change, residual, gamma, rho, lost, owed):
        ref[...] = jnp.zeros_like(ref)
    lhs = probe[0, :, :, SIDE:].reshape(m, acts)
    for side in (1, 0):
        for i in range(BLOCKS):
            load(side, i).wait()
        part = lax.dot_general(
            lhs, jac[side], (((1,), (1,)), ((), ())), preferred_element_type=f32
        )
        if side == 1:
            ipart[0] = part.astype(bf16)
            core_sum(0).start()
            send_scalars(0, 0, [])
        else:
            qown[0] = part
    join_cores(0, 0)

    def turn(i, carry):
        for side in range(2):
            at = pl.multiple_of(i * block, block)
            jact[side, :, pl.ds(at, block)] = jac[side, pl.ds(at, block), :].T
        return carry

    lax.fori_loop(0, BLOCKS, turn, 0)

    def turn_half(t, carry):
        here, there = lax.rem(t + 1, 2), lax.rem(t, 2)
        k_here = (t + 1) // 2 - 1
        k_there = t // 2

        @pl.when(t >= 2)
        def _():
            join_cores(here, k_here)
            settle_step(here)

        @pl.when(jnp.logical_and(t >= 2, t <= 2 * last + 1))
        def _():
            update(there, k_there - 1)

        @pl.when(t == 2 * last + 2)
        def _():
            finish(0)

        take_image(here, k_here)

        @pl.when(t <= 2 * last)
        def _():
            make_back(here)

        @pl.when(t > 2 * last)
        def _():
            send_kappa(here)

        @pl.when(t <= 2 * last + 1)
        def _():
            make_image(there, k_there)

        return carry

    lax.fori_loop(1, 2 * last + 3, turn_half, 0)
    finish(1)


def kernel_shards(nominal_field, sensitivity, aberrations, jacobian, tile_mask, regul, initial_commands):
    f32, bf16 = jnp.float32, jnp.bfloat16
    components, pixels, acts = jacobian.shape[1:]
    rows = components * pixels
    half = pixels
    reals = initial_commands.shape[0]
    n = lax.axis_size("section")
    m = reals // STREAMS
    mo = m // OWNERS
    core = lax.rem(lax.axis_index("section"), 2)
    mine = (jnp.arange(components) == core).astype(bf16)
    base = lax.dot_general(
        aberrations[:, :, None] * mine,
        sensitivity[0],
        (((1, 2), (0, 1)), ((), ())),
        preferred_element_type=f32,
    )
    vmem = pl.BlockSpec(memory_space=pltpu.VMEM)
    dma = pltpu.SemaphoreType.DMA
    commands, field = pl.pallas_call(
        functools.partial(control_kernel, n),
        out_shape=(
            jax.ShapeDtypeStruct((reals, acts), f32),
            jax.ShapeDtypeStruct((reals, components, pixels), f32),
        ),
        in_specs=[
            pl.BlockSpec(memory_space=pl.ANY),
            vmem,
            vmem,
            vmem,
            pl.BlockSpec(memory_space=pltpu.SMEM),
            vmem,
        ],
        out_specs=(vmem, vmem),
        scratch_shapes=[
            pltpu.VMEM((2, half, acts), bf16),
            pltpu.VMEM((2, acts, half), bf16),
            pltpu.VMEM((STREAMS, OWNERS, mo, SIDE + acts), bf16),
            pltpu.VMEM((STREAMS, OWNERS, mo, SIDE + acts), bf16),
            pltpu.VMEM((STREAMS, n - 1, mo, SIDE + acts), bf16),
            pltpu.VMEM((STREAMS, m, half), bf16),
            pltpu.VMEM((STREAMS, m, half), bf16),
            pltpu.VMEM((STREAMS, m, half), bf16),
            pltpu.VMEM((2, STREAMS, m, half), bf16),
            pltpu.VMEM((STREAMS, 2, m, half), bf16),
            pltpu.VMEM((STREAMS, m, half), f32),
            pltpu.VMEM((STREAMS, m, half), f32),
            pltpu.VMEM((STREAMS, m, half), f32),
            pltpu.VMEM((STREAMS, OWNERS, mo, acts), f32),
            pltpu.VMEM((STREAMS, OWNERS, mo, acts), f32),
            pltpu.VMEM((STREAMS, mo, acts), f32),
            pltpu.VMEM((m, max(2 * half, acts)), f32),
            pltpu.VMEM((STREAMS, OWNERS, mo, LANES), f32),
            pltpu.VMEM((STREAMS, OWNERS, mo, LANES), f32),
            pltpu.VMEM((n, 2, STREAMS, m, SIDE), bf16),
            pltpu.VMEM((STREAMS, 2, m, half), f32),
            pltpu.VMEM((STREAMS, OWNERS, mo, acts), f32),
            pltpu.VMEM((STREAMS, OWNERS, mo, acts), f32),
            pltpu.VMEM((STREAMS, OWNERS, mo, acts), bf16),
            pltpu.VMEM((STREAMS, n - 1, mo, acts), bf16),
            pltpu.VMEM((1, half), f32),
            pltpu.VMEM((2, n, STREAMS, m, LANES), f32),
            dma((2, BLOCKS)),
            dma((STREAMS,)),
            dma((STREAMS,)),
            dma((2, STREAMS)),
            dma((2, STREAMS)),
            dma((STREAMS,)),
            dma((STREAMS,)),
            dma((STREAMS, CHUNKS, OWNERS)),
            dma((STREAMS, CHUNKS, n - 1)),
            dma((STREAMS, CHUNKS, n - 1)),
            dma((STREAMS, CHUNKS, OWNERS)),
            dma((STREAMS, 2 * n - 1)),
            dma((STREAMS, 2 * n - 1)),
            dma((STREAMS, 2)),
            dma((STREAMS, 2)),
            dma((STREAMS, OWNERS)),
            dma((STREAMS, n - 1)),
            dma((2, STREAMS, n - 1)),
            dma((2, STREAMS, n - 1)),
        ],
        compiler_params=pltpu.CompilerParams(
            collective_id=0, has_side_effects=True, vmem_limit_bytes=48 * 1024 * 1024
        ),
        name="control_loop",
    )(
        jacobian.reshape(rows, acts),
        base,
        initial_commands,
        regul[None, :],
        tile_mask,
        nominal_field[0],
    )
    return commands, field.reshape(reals, 1, components, pixels)


def solution(mesh):
    placed = (
        P("wave", None, None),
        P("wave", None, None, None),
        P("groups", None),
        P("wave", None, None, "section"),
        P("wave", None),
        P("section"),
        P("groups", "section"),
    )

    def choose(*args):
        n, waves = mesh.shape["section"], mesh.shape["wave"]
        reals = args[6].shape[0]
        acts = args[3].shape[3]
        pixels = args[3].shape[2]
        fits = (
            n == 4
            and waves == 4
            and args[3].shape[1] == 2
            and reals % (16 * STREAMS * OWNERS) == 0
            and acts % (LANES * 16) == 0
            and pixels % (LANES * args[4].shape[1]) == 0
            and 2 * pixels * acts <= 2048 * 2048
            and reals <= 64
        )
        return (kernel_shards if fits else general_shards)(*args)

    return jax.shard_map(
        choose,
        mesh=mesh,
        in_specs=placed,
        out_specs=(P("groups", "section"), P("groups", "wave", None, None)),
        check_vma=False,
    )
```

```python
import functools

import jax
import jax.numpy as jnp
from jax import lax
from jax.experimental import pallas as pl
from jax.experimental.pallas import tpu as pltpu
from jax.sharding import PartitionSpec as P

ITERS = 2
CG = 5
LANES = 128
CHUNKS = 2
STREAMS = 2
OWNERS = 2
SIDE = 128
BLOCKS = 4
PAD = 128
FIRST = 6

epsilon = 1e-06


def to_section_image(command_bf, jac_block):
    partial_value = lax.dot_general(
        command_bf, jac_block, (((1,), (1,)), ((), ())), preferred_element_type=jnp.float32
    )
    return lax.psum_scatter(
        partial_value.astype(jnp.bfloat16), "section", scatter_dimension=1, tiled=True
    ).astype(jnp.float32)


def back_of(masked_share, jac_block):
    masked_bf = lax.all_gather(masked_share, "section", axis=1, tiled=True)
    partial_value = jnp.dot(masked_bf, jac_block, preferred_element_type=jnp.float32)
    owned = lax.psum_scatter(
        partial_value.astype(jnp.bfloat16), "wave", scatter_dimension=1, tiled=True
    ).astype(jnp.float32)
    return lax.all_gather(owned, "wave", axis=1, tiled=True)


def reduce_scalars(values):
    return lax.psum(values, "section")


def general_shards(nominal_field, sensitivity, aberrations, jacobian, tile_mask, regul, initial_commands):
    components = jacobian.shape[1]
    pixels = jacobian.shape[2]
    block_width = jacobian.shape[3]
    row_count = components * pixels
    share_rows = row_count // lax.axis_size("section")
    row_start = lax.axis_index("section") * share_rows
    jac_block = jacobian.reshape(row_count, block_width)
    tile_count = tile_mask.shape[1]
    weight_full = jnp.broadcast_to(
        tile_mask[0].astype(jnp.float32)[None, :, None],
        (components, tile_count, pixels // tile_count),
    ).reshape(1, row_count)
    weight = lax.dynamic_slice_in_dim(weight_full, row_start, share_rows, 1)
    mode_count = sensitivity.shape[1]
    sens_share = lax.dynamic_slice_in_dim(
        sensitivity.reshape(mode_count, row_count), row_start, share_rows, 1
    )
    nominal_share = lax.dynamic_slice_in_dim(
        nominal_field.reshape(1, row_count), row_start, share_rows, 1
    )
    field_now = nominal_share + jnp.dot(aberrations, sens_share, preferred_element_type=jnp.float32)
    commands = initial_commands
    field_now = field_now + to_section_image(commands.astype(jnp.bfloat16), jac_block)
    for iteration in range(ITERS):
        residual = -back_of((weight * field_now).astype(jnp.bfloat16), jac_block)
        direction = residual
        change = jnp.zeros_like(residual)
        field_step = jnp.zeros_like(field_now)
        norm_now = reduce_scalars(jnp.sum(residual * residual, axis=1))
        for inner_step in range(CG):
            image_now = to_section_image(direction.astype(jnp.bfloat16), jac_block)
            applied = (
                back_of((weight * image_now).astype(jnp.bfloat16), jac_block)
                + regul[None, :] * direction
            )
            curvature = reduce_scalars(jnp.sum(direction * applied, axis=1))
            step_len = norm_now / (curvature + epsilon)
            residual = residual - step_len[:, None] * applied
            norm_next = reduce_scalars(jnp.sum(residual * residual, axis=1))
            change = change + step_len[:, None] * direction
            field_step = field_step + step_len[:, None] * image_now
            direction = residual + (norm_next / (norm_now + epsilon))[:, None] * direction
            norm_now = norm_next
        commands = commands + change
        field_now = field_now + field_step
    whole_field = lax.all_gather(
        field_now.astype(jnp.bfloat16), "section", axis=1, tiled=True
    ).astype(field_now.dtype)
    return (commands, whole_field.reshape(whole_field.shape[0], 1, components, pixels))


def control_kernel(
    n,
    jac_hbm,
    base_ref,
    start_ref,
    regul_ref,
    tile_ref,
    nominal_ref,
    cmd_ref,
    out_ref,
    jac,
    jact,
    probe,
    wpart,
    wrecv,
    ipart,
    crecv,
    xsend,
    xrecv,
    masked,
    img,
    field,
    qown,
    direction,
    change,
    residual,
    acc,
    gamma,
    rho,
    kappas,
    other,
    lost,
    owed,
    opart,
    orecv,
    weight_ref,
    scal,
    jac_sem,
    cs_s,
    cs_r,
    xx_s,
    xx_r,
    cg_s,
    cg_r,
    ws_s,
    ws_r,
    ag_s,
    ag_r,
    fin_s,
    fin_r,
    out_s,
    out_r,
    ow_s,
    ow_r,
    sc_s,
    sc_r,
):
    f32, bf16 = jnp.float32, jnp.bfloat16
    half, acts = jac.shape[1:]
    mo = probe.shape[2]
    m = OWNERS * mo
    cut = [0, acts * FIRST // 16, acts]
    last = ITERS * CG
    sec, wav = lax.axis_index("section"), lax.axis_index("wave")
    core = lax.rem(sec, 2)
    sibling = {"section": sec + 1 - 2 * core}
    across = {"section": lax.rem(sec + 2, n)}
    first_owner = n // 2 - 1
    owners = [first_owner + o for o in range(OWNERS)]
    is_owner = jnp.logical_and(wav >= owners[0], wav <= owners[-1])
    far = jnp.where(wav <= first_owner, 1, 0)
    mine = jnp.clip(wav - first_owner, 0, OWNERS - 1)
    peers = range(n - 1)
    wav_peer = [{"wave": lax.rem(wav + k + 1, n)} for k in peers]

    block = half // BLOCKS

    def load(side, i):
        at = pl.multiple_of((core if side == 0 else 1 - core) * half + i * block, block)
        return pltpu.make_async_copy(
            jac_hbm.at[pl.ds(at, block)], jac.at[side, pl.ds(i * block, block)], jac_sem.at[side, i]
        )

    for side in (1, 0):
        for i in range(BLOCKS):
            load(side, i).start()
    barrier = pltpu.get_barrier_semaphore()
    slanted = [{"wave": lax.rem(wav + k + 1, n), **sibling} for k in peers]
    final_peer = slanted + wav_peer + [sibling]
    opposite = {"section": lax.rem(sec + 3 - 2 * core, n)}
    greeted = final_peer + [across, opposite]
    for p in greeted:
        pl.semaphore_signal(barrier, inc=1, device_id=p, device_id_type=pl.DeviceIdType.MESH)
    pl.semaphore_wait(barrier, len(greeted))

    def remote(src, dst, ss, rs, device):
        return pltpu.make_async_remote_copy(
            src_ref=src, dst_ref=dst, send_sem=ss, recv_sem=rs,
            device_id=device, device_id_type=pl.DeviceIdType.MESH,
        )

    def part_cols(c):
        low = 0 if c == 0 else SIDE + cut[c]
        return pl.ds(low, SIDE + cut[c + 1] - low)

    def core_sum(s):
        return remote(ipart.at[s], crecv.at[s], cs_s.at[s], cs_r.at[s], sibling)

    def x_sum(s, slot):
        return remote(xsend.at[s], xrecv.at[slot, s], xx_s.at[slot, s], xx_r.at[slot, s], across)

    def scal_copy(s, slot, k):
        return remote(
            scal.at[slot, sec, s],
            scal.at[slot, sec, s],
            sc_s.at[slot, s, k],
            sc_r.at[slot, s, k],
            {"section": lax.rem(sec + k + 1, n)},
        )

    def core_share(s):
        return remote(masked.at[s, 0], masked.at[s, 1], cg_s.at[s], cg_r.at[s], sibling)

    def to_owner(s, c, o):
        owner = first_owner + o
        k = lax.rem(wav - owner + n - 1 + n, n)
        return remote(
            wpart.at[s, o, :, part_cols(c)],
            wrecv.at[s, k, :, part_cols(c)],
            ws_s.at[s, c, o],
            ws_r.at[s, c, k],
            {"wave": owner},
        )

    def owed_copy(s, o):
        owner = first_owner + o
        k = lax.rem(wav - owner + n - 1 + n, n)
        return remote(
            opart.at[s, o], orecv.at[s, k], ow_s.at[s, o], ow_r.at[s, k], {"wave": owner}
        )

    def owed_at(s, k):
        return remote(opart.at[s, 0], orecv.at[s, k], ow_s.at[s, 0], ow_r.at[s, k], wav_peer[0])

    def at_owner(s, c, k):
        return remote(
            wpart.at[s, 0, :, part_cols(c)],
            wrecv.at[s, k, :, part_cols(c)],
            ws_s.at[s, c, 0],
            ws_r.at[s, c, k],
            wav_peer[0],
        )

    def from_owner(s, c, o, k):
        return remote(
            probe.at[s, o, :, part_cols(c)],
            probe.at[s, o, :, part_cols(c)],
            ag_s.at[s, c, k],
            ag_r.at[s, c, o],
            wav_peer[k],
        )

    def kappa_copy(s, k):
        return remote(
            kappas.at[wav, core, s],
            kappas.at[wav, core, s],
            fin_s.at[s, k],
            fin_r.at[s, k],
            final_peer[k],
        )

    def out_copy(s, at):
        return remote(
            (field, img)[at].at[s], other.at[s, at], out_s.at[s, at], out_r.at[s, at], sibling
        )

    def row_sum(values):
        return jnp.sum(values, axis=1, keepdims=True)

    def pack(values):
        lane = lax.broadcasted_iota(jnp.int32, (values[0].shape[0], SIDE), 1)
        packed = jnp.zeros(lane.shape, f32)
        for at, value in enumerate(values):
            rest = value
            for piece in range(3):
                top = rest.astype(bf16).astype(f32)
                rest = rest - top
                packed = jnp.where(lane == 3 * at + piece, top, packed)
        return packed.astype(bf16)

    def spread(column):
        return jnp.broadcast_to(column, (column.shape[0], LANES))

    def dot(lhs, rhs):
        padded = jnp.concatenate([lhs, jnp.zeros((PAD - m, lhs.shape[1]), bf16)], axis=0)
        return jnp.dot(padded, rhs, preferred_element_type=f32)[:m]

    def send_scalars(s, k, sums):
        lane = lax.broadcasted_iota(jnp.int32, (m, LANES), 1)
        packed = jnp.zeros((m, LANES), f32)
        for at, value in enumerate(sums):
            packed = jnp.where(lane == at, value, packed)
        slot = lax.rem(k, 2)
        scal[slot, sec, s] = packed
        for p in peers:
            scal_copy(s, slot, p).start()

    def make_image(s, k):
        def arrive(c):
            @pl.when(k > 0)
            def _():
                for o in range(OWNERS):
                    @pl.when(wav != owners[o])
                    def _():
                        from_owner(s, c, o, 0).wait_recv()

        def scalars(c, lhs):
            cols = slice(cut[c], cut[c + 1])
            wide = lhs.astype(f32)
            scaled = regul_ref[:, cols] * wide
            along = direction[s, :, :, cols].reshape(m, cut[c + 1] - cut[c])
            return [row_sum(wide * wide), row_sum(scaled * wide), row_sum(scaled * along)]

        sums = None
        for c in range(CHUNKS):
            arrive(c)
            lhs = probe[s, :, :, SIDE + cut[c]:SIDE + cut[c + 1]].reshape(m, cut[c + 1] - cut[c])
            for side in (1, 0):
                part = dot(lhs, jact[side, cut[c]:cut[c + 1], :])
                cols = slice(side * half, (side + 1) * half)
                if c:
                    part = acc[:, cols] + part
                if c < CHUNKS - 1:
                    acc[:, cols] = part
                elif side == 1:
                    ipart[s] = part.astype(bf16)
                    core_sum(s).start()
                else:
                    qown[s] = part
                if side == 1:
                    more = scalars(c, lhs)
                    sums = more if sums is None else [x + y for x, y in zip(sums, more)]
                    if c == CHUNKS - 1:
                        send_scalars(s, k, sums)
        step = row_sum(probe[s, :, :, 0:SIDE].reshape(m, SIDE).astype(f32))
        field[s] = field[s] + step * img[s]
        step = step.reshape(OWNERS, mo, 1)
        change[s] = change[s] + step * direction[s]
        owed[s] = owed[s] + step * lost[s]

    def settle(s):
        for p in peers:
            owed_at(s, p).wait_recv()
        total = opart[s, mine].astype(f32)
        for p in peers:
            total = total + orecv[s, p].astype(f32)
        residual[s] = residual[s] - total

    def join_cores(s, k):
        core_sum(s).wait()
        xsend[s] = (qown[s] + crecv[s].astype(f32)).astype(bf16)
        x_sum(s, lax.rem(k, 2)).start()

        @pl.when(k == CG)
        def _():
            opart[s] = owed[s].astype(bf16)

    def take_image(s, k):
        slot = lax.rem(k, 2)
        for p in peers:
            scal_copy(s, slot, p).wait()
        lanes = scal[slot, 0, s]
        for at in range(1, n):
            lanes = lanes + scal[slot, at, s]
        norm, aa, bb = [lanes[:, at:at + 1] for at in range(3)]
        norm_before = gamma[s].reshape(m, LANES)[:, 0:1]
        rho_before = rho[s].reshape(m, LANES)[:, 0:1]
        ratio = norm / (norm_before + epsilon)
        ratio = jnp.where(lax.rem(k, CG) == 1, 0.0, ratio)
        ratio = jnp.where(k == 0, 1.0, ratio)
        rho_now = jnp.maximum(aa + 2.0 * ratio * bb + ratio * ratio * rho_before, 0.0)
        gamma[s] = spread(norm).reshape(OWNERS, mo, LANES)
        rho[s] = spread(rho_now).reshape(OWNERS, mo, LANES)
        fresh = jnp.where(k == 0, 0.0, 1.0)
        direction[s] = (
            fresh * probe[s, :, :, SIDE:].astype(f32) + ratio.reshape(OWNERS, mo, 1) * direction[s]
        )
        img[s] = ratio * img[s]
        @pl.when(k > 0)
        def _():
            for c in range(CHUNKS):
                to_owner(s, c, far).wait_send()

                @pl.when(jnp.logical_not(is_owner))
                def _():
                    to_owner(s, c, 1 - far).wait_send()

            @pl.when(is_owner)
            def _():
                for c in range(CHUNKS):
                    for p in peers:
                        from_owner(s, c, mine, p).wait_send()

            @pl.when(k == CG + 1)
            def _():
                owed_copy(s, far).wait_send()

                @pl.when(jnp.logical_not(is_owner))
                def _():
                    owed_copy(s, 1 - far).wait_send()

        x_sum(s, slot).wait()
        now = xsend[s].astype(f32) + xrecv[slot, s].astype(f32) + img[s]
        img[s] = now
        kept = (weight_ref[...] * now).astype(bf16)
        masked[s, 0] = kept

        @pl.when(k < last)
        def _():
            core_share(s).start()

        @pl.when(k == CG)
        def _():
            owed_copy(s, far).start()

            @pl.when(jnp.logical_not(is_owner))
            def _():
                owed_copy(s, 1 - far).start()

    def square(s, side):
        wide = masked[s, side].astype(f32)
        return row_sum(wide * wide)

    def make_back(s):
        lhs = masked[s, 0]
        for c in range(CHUNKS):
            cols = slice(cut[c], cut[c + 1])
            acc[:, cols] = dot(lhs, jac[0, :, cols])
        kappa = square(s, 0)
        core_share(s).wait()
        kappa = pack([kappa + square(s, 1)])
        wpart[s, :, :, 0:SIDE] = kappa.reshape(OWNERS, mo, SIDE)
        lhs = masked[s, 1]
        for c in range(CHUNKS):
            cols = slice(cut[c], cut[c + 1])
            part = acc[:, cols] + dot(lhs, jac[1, :, cols])
            sent = part.astype(bf16)
            wpart[s, :, :, SIDE + cut[c]:SIDE + cut[c + 1]] = sent.reshape(OWNERS, mo, cut[c + 1] - cut[c])
            to_owner(s, c, far).start()

            @pl.when(jnp.logical_not(is_owner))
            def _():
                to_owner(s, c, 1 - far).start()

            lost[s, :, :, cols] = (part - sent.astype(f32)).reshape(OWNERS, mo, cut[c + 1] - cut[c])

    def update(s, k):
        @pl.when(is_owner)
        def _():
            again = jnp.where(k == CG, 1.0, 0.0)

            @pl.when(k == CG)
            def _():
                settle(s)

            for c in range(CHUNKS):
                for p in peers:
                    at_owner(s, c, p).wait_recv()
                if c == 0:
                    kappa = wpart[s, mine, :, 0:SIDE].astype(f32)
                    for p in peers:
                        kappa = kappa + wrecv[s, p, :, 0:SIDE].astype(f32)
                    kappa = row_sum(kappa)
                    norm, rho_now = gamma[s, mine][:, 0:1], rho[s, mine][:, 0:1]
                    step = norm / (kappa + rho_now + epsilon)
                    step = jnp.where(k == 0, 1.0, step)
                    probe[s, mine, :, 0:SIDE] = pack([step])
                cols = slice(cut[c], cut[c + 1])
                wide = slice(SIDE + cut[c], SIDE + cut[c + 1])
                total = wpart[s, mine, :, wide].astype(f32)
                for p in peers:
                    total = total + wrecv[s, p, :, wide].astype(f32)
                along = direction[s, mine, :, cols]
                weight = regul_ref[:, cols]
                after = residual[s, :, cols] - step * (total + weight * along)
                after = after + again * (weight * (change[s, mine, :, cols] + step * along))
                residual[s, :, cols] = after
                probe[s, mine, :, wide] = after.astype(bf16)
                for p in (1, 0, 2):
                    from_owner(s, c, mine, p).start()

    def send_kappa(s):
        for at in range(2):
            out_copy(s, at).start()
        kappas[wav, core, s] = pack([square(s, 0)])
        for p in range(len(final_peer)):
            kappa_copy(s, p).start()

    def finish(s):
        for p in range(len(final_peer)):
            kappa_copy(s, p).wait()
        kappa = jnp.zeros((m, SIDE), f32)
        for w in range(n):
            for c in range(2):
                kappa = kappa + kappas[w, c, s].astype(f32)
        step = gamma[s].reshape(m, LANES)[:, 0:1]
        step = step / (row_sum(kappa) + rho[s].reshape(m, LANES)[:, 0:1] + epsilon)
        rows = pl.ds(s * m, m)
        moved = change[s] + step.reshape(OWNERS, mo, 1) * direction[s]
        cmd_ref[rows, :] = start_ref[rows, :] + moved.reshape(m, acts)
        for at in range(2):
            out_copy(s, at).wait()
        here = field[s] + step * img[s]
        there = other[s, 0] + step * other[s, 1]
        out_ref[rows, 0, :] = jnp.where(core == 0, here, there)
        out_ref[rows, 1, :] = jnp.where(core == 0, there, here)

    for s in range(STREAMS):
        probe[s, :, :, 0:SIDE] = jnp.zeros((OWNERS, mo, SIDE), bf16)
        probe[s, :, :, SIDE:] = start_ref[s * m:(s + 1) * m, :].astype(bf16).reshape(OWNERS, mo, acts)
        nominal = jnp.where(core == 0, nominal_ref[0:1, :], nominal_ref[1:2, :])
        img[s] = nominal + base_ref[s * m:(s + 1) * m, :]
    tiles = tile_ref.shape[1]
    wide = half // tiles
    for tile in range(tiles):
        weight_ref[:, tile * wide:(tile + 1) * wide] = jnp.full(
            (1, wide), tile_ref[0, tile].astype(f32), f32
        )
    for ref in (field, direction, change, residual, gamma, rho, lost, owed):
        ref[...] = jnp.zeros_like(ref)
    lhs = probe[0, :, :, SIDE:].reshape(m, acts)
    for side in (1, 0):
        for i in range(BLOCKS):
            load(side, i).wait()
        part = lax.dot_general(
            lhs, jac[side], (((1,), (1,)), ((), ())), preferred_element_type=f32
        )
        if side == 1:
            ipart[0] = part.astype(bf16)
            core_sum(0).start()
            send_scalars(0, 0, [])
        else:
            qown[0] = part
    join_cores(0, 0)

    def turn(i, carry):
        for side in range(2):
            at = pl.multiple_of(i * block, block)
            jact[side, :, pl.ds(at, block)] = jac[side, pl.ds(at, block), :].T
        return carry

    lax.fori_loop(0, BLOCKS, turn, 0)

    def turn_half(t, carry):
        here, there = lax.rem(t + 1, 2), lax.rem(t, 2)
        k_here = (t + 1) // 2 - 1
        k_there = t // 2

        @pl.when(t >= 2)
        def _():
            join_cores(here, k_here)

        @pl.when(jnp.logical_and(t >= 2, t <= 2 * last + 1))
        def _():
            update(there, k_there - 1)

        @pl.when(t == 2 * last + 2)
        def _():
            finish(0)

        take_image(here, k_here)

        @pl.when(t <= 2 * last)
        def _():
            make_back(here)

        @pl.when(t > 2 * last)
        def _():
            send_kappa(here)

        @pl.when(t <= 2 * last + 1)
        def _():
            make_image(there, k_there)

        return carry

    lax.fori_loop(1, 2 * last + 3, turn_half, 0)
    finish(1)


def kernel_shards(nominal_field, sensitivity, aberrations, jacobian, tile_mask, regul, initial_commands):
    f32, bf16 = jnp.float32, jnp.bfloat16
    components, pixels, acts = jacobian.shape[1:]
    rows = components * pixels
    half = pixels
    reals = initial_commands.shape[0]
    n = lax.axis_size("section")
    m = reals // STREAMS
    mo = m // OWNERS
    core = lax.rem(lax.axis_index("section"), 2)
    mine = (jnp.arange(components) == core).astype(bf16)
    base = lax.dot_general(
        aberrations[:, :, None] * mine,
        sensitivity[0],
        (((1, 2), (0, 1)), ((), ())),
        preferred_element_type=f32,
    )
    vmem = pl.BlockSpec(memory_space=pltpu.VMEM)
    dma = pltpu.SemaphoreType.DMA
    commands, field = pl.pallas_call(
        functools.partial(control_kernel, n),
        out_shape=(
            jax.ShapeDtypeStruct((reals, acts), f32),
            jax.ShapeDtypeStruct((reals, components, pixels), f32),
        ),
        in_specs=[
            pl.BlockSpec(memory_space=pl.ANY),
            vmem,
            vmem,
            vmem,
            pl.BlockSpec(memory_space=pltpu.SMEM),
            vmem,
        ],
        out_specs=(vmem, vmem),
        scratch_shapes=[
            pltpu.VMEM((2, half, acts), bf16),
            pltpu.VMEM((2, acts, half), bf16),
            pltpu.VMEM((STREAMS, OWNERS, mo, SIDE + acts), bf16),
            pltpu.VMEM((STREAMS, OWNERS, mo, SIDE + acts), bf16),
            pltpu.VMEM((STREAMS, n - 1, mo, SIDE + acts), bf16),
            pltpu.VMEM((STREAMS, m, half), bf16),
            pltpu.VMEM((STREAMS, m, half), bf16),
            pltpu.VMEM((STREAMS, m, half), bf16),
            pltpu.VMEM((2, STREAMS, m, half), bf16),
            pltpu.VMEM((STREAMS, 2, m, half), bf16),
            pltpu.VMEM((STREAMS, m, half), f32),
            pltpu.VMEM((STREAMS, m, half), f32),
            pltpu.VMEM((STREAMS, m, half), f32),
            pltpu.VMEM((STREAMS, OWNERS, mo, acts), f32),
            pltpu.VMEM((STREAMS, OWNERS, mo, acts), f32),
            pltpu.VMEM((STREAMS, mo, acts), f32),
            pltpu.VMEM((m, max(2 * half, acts)), f32),
            pltpu.VMEM((STREAMS, OWNERS, mo, LANES), f32),
            pltpu.VMEM((STREAMS, OWNERS, mo, LANES), f32),
            pltpu.VMEM((n, 2, STREAMS, m, SIDE), bf16),
            pltpu.VMEM((STREAMS, 2, m, half), f32),
            pltpu.VMEM((STREAMS, OWNERS, mo, acts), f32),
            pltpu.VMEM((STREAMS, OWNERS, mo, acts), f32),
            pltpu.VMEM((STREAMS, OWNERS, mo, acts), bf16),
            pltpu.VMEM((STREAMS, n - 1, mo, acts), bf16),
            pltpu.VMEM((1, half), f32),
            pltpu.VMEM((2, n, STREAMS, m, LANES), f32),
            dma((2, BLOCKS)),
            dma((STREAMS,)),
            dma((STREAMS,)),
            dma((2, STREAMS)),
            dma((2, STREAMS)),
            dma((STREAMS,)),
            dma((STREAMS,)),
            dma((STREAMS, CHUNKS, OWNERS)),
            dma((STREAMS, CHUNKS, n - 1)),
            dma((STREAMS, CHUNKS, n - 1)),
            dma((STREAMS, CHUNKS, OWNERS)),
            dma((STREAMS, 2 * n - 1)),
            dma((STREAMS, 2 * n - 1)),
            dma((STREAMS, 2)),
            dma((STREAMS, 2)),
            dma((STREAMS, OWNERS)),
            dma((STREAMS, n - 1)),
            dma((2, STREAMS, n - 1)),
            dma((2, STREAMS, n - 1)),
        ],
        compiler_params=pltpu.CompilerParams(
            collective_id=0, has_side_effects=True, vmem_limit_bytes=48 * 1024 * 1024
        ),
        name="control_loop",
    )(
        jacobian.reshape(rows, acts),
        base,
        initial_commands,
        regul[None, :],
        tile_mask,
        nominal_field[0],
    )
    return commands, field.reshape(reals, 1, components, pixels)


def solution(mesh):
    placed = (
        P("wave", None, None),
        P("wave", None, None, None),
        P("groups", None),
        P("wave", None, None, "section"),
        P("wave", None),
        P("section"),
        P("groups", "section"),
    )

    def choose(*args):
        n, waves = mesh.shape["section"], mesh.shape["wave"]
        reals = args[6].shape[0]
        acts = args[3].shape[3]
        pixels = args[3].shape[2]
        fits = (
            n == 4
            and waves == 4
            and args[3].shape[1] == 2
            and reals % (16 * STREAMS * OWNERS) == 0
            and acts % (LANES * 16) == 0
            and pixels % (LANES * args[4].shape[1]) == 0
            and 2 * pixels * acts <= 2048 * 2048
            and reals <= 64
        )
        return (kernel_shards if fits else general_shards)(*args)

    return jax.shard_map(
        choose,
        mesh=mesh,
        in_specs=placed,
        out_specs=(P("groups", "section"), P("groups", "wave", None, None)),
        check_vma=False,
    )
```
